32 devices in a mesh: shard: 4 (over z), context: 2 (over y), tensor: 4 (over x, core).
Axes of the slice: x: 2, y: 2, z: 4, core: 2. Of those that a mesh axis runs over, the one named last changes fastest.
Arguments:
- hidden_in: bfloat16 [4, 1024, 2048], P('shard', 'context'), may hold values from -6 to 6
- cotangent: bfloat16 [4, 1024, 2048], P('shard', 'context'), may hold values from -6 to 6
- segment_ids: int32 [4, 1024], P('shard'), may hold values from 0 to 10, as said below
- positions: int32 [4, 1024], P('shard', 'context'), may hold values from 0 to 999, as said below
- attention_gain: bfloat16 [2048], P('shard'), may hold values from 0.5 to 1.5
- query_weight: bfloat16 [2048, 2048], P('shard', 'tensor'), may hold values from -0.125 to 0.125
- key_weight: bfloat16 [2048, 512], P('shard', 'tensor'), may hold values from -0.125 to 0.125
- value_weight: bfloat16 [2048, 512], P('shard', 'tensor'), may hold values from -0.125 to 0.125
- output_weight: bfloat16 [2048, 2048], P('tensor', 'shard'), may hold values from -0.75 to 0.75
- feed_gain: bfloat16 [2048], P('shard'), may hold values from 0.5 to 1.5
- gate_weight: bfloat16 [2048, 8192], P('shard', 'tensor'), may hold values from -0.125 to 0.125
- up_weight: bfloat16 [2048, 8192], P('shard', 'tensor'), may hold values from -0.125 to 0.125
- down_weight: bfloat16 [8192, 2048], P('tensor', 'shard'), may hold values from -0.0625 to 0.0625
Outputs:
- layer_out: bfloat16 [4, 1024, 2048], P('shard', ('context', 'tensor'))
- grad_input: float32 [4, 1024, 2048], P('shard', ('context', 'tensor'))
- grad_attention_gain: float32 [2048], P('shard')
- grad_query: float32 [2048, 2048], P('shard', 'tensor')
- grad_key: float32 [2048, 512], P('shard', 'tensor')
- grad_value: float32 [2048, 512], P('shard', 'tensor')
- grad_output: float32 [2048, 2048], P('tensor', 'shard')
- grad_feed_gain: float32 [2048], P('shard')
- grad_gate: float32 [2048, 8192], P('shard', 'tensor')
- grad_up: float32 [2048, 8192], P('shard', 'tensor')
- grad_down: float32 [8192, 2048], P('tensor', 'shard')
The draws below stay inside these ranges and needn't reach their ends.
Inputs may be any that keep to these rules, and one draw needn't show every extreme that they name: `segment_ids`: segment ids count the documents of a sequence from 0 in order; every document holds 100 to 1000 tokens (rounded down, at least 1), except the last of a sequence, which may be shorter. `positions`: positions count the tokens of each document from 0 at its first token.
All inputs are finite; a program needn't handle non-finite values.
Results may differ from the reference program's by a relative error of at most 0.018.
Values may be sent and summed in bfloat16 or wider, within the bound.
No kernel may reach another device: no remote copies, remote signals or barrier semaphores. Data moves between devices by JAX's collectives and lax.ppermute only.
A program may use at most 256 MiB of HBM per device.

```python
import jax
import jax.numpy as jnp
from jax import lax

D = 2048
HEADS = 32
KV_HEADS = 8
HEAD = 64
FF = 8192
LEN = 1024
SEQS = 4


def document_layout(key):
    base = jax.random.fold_in(key, 11)
    shortest = max(LEN * 25 // 256, 1)
    longest = LEN * 125 // 128
    count = LEN // shortest + 1
    sizes = jax.random.randint(base, (SEQS, count), shortest, longest + 1, dtype=jnp.int32)
    sizes = sizes.at[0, 0].set(longest)
    sizes = sizes.at[1, :].set(shortest)
    ends = jnp.cumsum(sizes, axis=1)
    token = jnp.arange(LEN, dtype=jnp.int32)
    segment = jnp.sum((ends[:, None, :] <= token[None, :, None]).astype(jnp.int32), axis=2)
    starts = ends - sizes
    first = jnp.take_along_axis(starts, segment, axis=1)
    return (segment.astype(jnp.int32), (token[None, :] - first).astype(jnp.int32))


def draw_segment_ids(key, part):
    return document_layout(key)[0]


def draw_positions(key, part):
    return document_layout(key)[1]


def block_scale(rng, shape, pieces, least, largest):
    level = 1.0
    for dim, shards_of in pieces:
        steps = jax.random.uniform(jax.random.fold_in(jax.random.fold_in(rng, 6), dim), (shards_of,), jnp.float32, least / len(pieces), largest / len(pieces))
        level = level * jnp.repeat(jnp.exp(steps), shape[dim] // shards_of).reshape((-1,) + (1,) * (len(shape) - 1 - dim))
    return level


def noise(rng, shape, scale, limit, cuts=(), held_as=jnp.bfloat16):
    array = jax.random.normal(rng, shape, jnp.float32) * scale
    if len(cuts) > 0:
        array = block_scale(rng, shape, cuts, -0.22, 0.18) * array
    return jnp.clip(array, min=-limit, max=limit).astype(held_as)


def setup_inputs(seed: int = 0) -> dict:
    key_of = jax.random.split(jax.random.key(seed), 14)
    hidden_in = noise(key_of[0], (SEQS, LEN, D), 1.0, 6.0, ((0, 4), (1, 2)))
    cotangent = noise(key_of[1], (SEQS, LEN, D), 1.0, 6.0, ((0, 4), (1, 2)))
    segment_ids = draw_segment_ids(jax.random.fold_in(key_of[13], 71), 0)
    positions = draw_positions(jax.random.fold_in(key_of[13], 71), 0)
    attention_gain = jnp.clip(1.0 + 0.1 * jax.random.normal(key_of[4], (D,), jnp.float32), 0.5, 1.5).astype(jnp.bfloat16)
    query_weight = noise(key_of[5], (D, HEADS * HEAD), D ** -0.5, 0.125, ((0, 4), (1, 4)))
    key_weight = noise(key_of[6], (D, KV_HEADS * HEAD), D ** -0.5, 0.125, ((0, 4), (1, 4)))
    value_weight = noise(key_of[7], (D, KV_HEADS * HEAD), D ** -0.5, 0.125, ((0, 4), (1, 4)))
    output_weight = noise(key_of[8], (HEADS * HEAD, D), (HEADS * HEAD // 32) ** -0.5, 0.75, ((0, 4), (1, 4)))
    feed_gain = jnp.clip(1.0 + 0.1 * jax.random.normal(key_of[9], (D,), jnp.float32), 0.5, 1.5).astype(jnp.bfloat16)
    gate_weight = noise(key_of[10], (D, FF), D ** -0.5, 0.125, ((0, 4), (1, 4)))
    up_weight = noise(key_of[11], (D, FF), D ** -0.5, 0.125, ((0, 4), (1, 4)))
    down_weight = noise(key_of[12], (FF, D), FF ** -0.5, 0.0625, ((0, 4), (1, 4)))
    return dict(hidden_in=hidden_in, cotangent=cotangent, segment_ids=segment_ids, positions=positions, attention_gain=attention_gain, query_weight=query_weight, key_weight=key_weight, value_weight=value_weight, output_weight=output_weight, feed_gain=feed_gain, gate_weight=gate_weight, up_weight=up_weight, down_weight=down_weight)


NORM_EPS = 1e-05
ROPE_BASE = 500000.0
MASKED = -1e+30

def matmul(left, right):
    return jnp.dot(left, right, preferred_element_type=jnp.float32)

def rms_forward(values, gain):
    inverse = lax.rsqrt(lax.optimization_barrier(jnp.mean(values * values, axis=-1, keepdims=True)) + NORM_EPS)
    normed = values * inverse
    return (normed * gain.astype(jnp.float32), normed, inverse)

def rms_backward(upstream, normed, inverse, gain):
    scaled = upstream * gain.astype(jnp.float32)
    result = inverse * (scaled - normed * lax.optimization_barrier(jnp.mean(scaled * normed, axis=-1, keepdims=True)))
    return (result, lax.optimization_barrier(jnp.sum(upstream * normed, axis=0)))

def rope_angles(positions):
    inverse_freq = ROPE_BASE ** (-(jnp.arange(HEAD // 2, dtype=jnp.float32) * 2.0 / HEAD))
    angles = positions.astype(jnp.float32)[:, None] * inverse_freq[None, :]
    return (jnp.cos(angles)[:, None, :], jnp.sin(angles)[:, None, :])

def rotate(tensor, cosine, sine_part, turn):
    first = tensor[..., :HEAD // 2]
    second = tensor[..., HEAD // 2:]
    return jnp.concatenate([first * cosine - turn * second * sine_part, second * cosine + turn * first * sine_part], axis=-1)

def block_mask(segment_row, row_start, block_rows):
    length = segment_row.shape[0]
    index = jnp.arange(length, dtype=jnp.int32)
    query_index = index[row_start:row_start + block_rows]
    query_segment = segment_row[row_start:row_start + block_rows]
    return (query_index[:, None] >= index[None, :]) & (query_segment[:, None] == segment_row[None, :])

def block_scores(query_block, keys_wide, allowed):
    scores = jnp.einsum('qkgd,tkd->kgqt', query_block, keys_wide) * HEAD ** (-0.5)
    return jnp.where(allowed[None, None], scores, MASKED)

def attention_forward(query_four, key_b, value_b, segment_row):
    length = query_four.shape[0]
    block_rows = min(512, length)
    keys_wide = key_b.astype(jnp.float32)
    values_wide = value_b.astype(jnp.float32)
    outputs = []
    totals = []
    for row_start in range(0, length, block_rows):
        query_block = query_four[row_start:row_start + block_rows].astype(jnp.float32)
        scores = block_scores(query_block, keys_wide, block_mask(segment_row, row_start, block_rows))
        log_total = jnp.log(lax.optimization_barrier(jnp.sum(jnp.exp(scores), axis=-1, keepdims=True)))
        weights_b = jnp.exp(scores - log_total).astype(jnp.bfloat16)
        attended = jnp.einsum('kgqt,tkd->qkgd', weights_b.astype(jnp.float32), values_wide).astype(jnp.bfloat16)
        outputs.append(attended)
        totals.append(log_total)
    return (jnp.concatenate(outputs, axis=0), totals)

def attention_backward(query_four, key_b, value_b, segment_row, attended_four, upstream_four, totals):
    length = query_four.shape[0]
    block_rows = min(512, length)
    keys_wide = key_b.astype(jnp.float32)
    values_wide = value_b.astype(jnp.float32)
    key_sum = jnp.zeros(key_b.shape, jnp.float32)
    value_sum = jnp.zeros(value_b.shape, jnp.float32)
    query_grads = []
    for block_index, row_start in enumerate(range(0, length, block_rows)):
        query_block = query_four[row_start:row_start + block_rows].astype(jnp.float32)
        upstream = upstream_four[row_start:row_start + block_rows].astype(jnp.float32)
        out_block = attended_four[row_start:row_start + block_rows].astype(jnp.float32)
        scores = block_scores(query_block, keys_wide, block_mask(segment_row, row_start, block_rows))
        probability = jnp.exp(scores - totals[block_index])
        weights_b = probability.astype(jnp.bfloat16).astype(jnp.float32)
        grad_probs = jnp.einsum('qkgd,tkd->kgqt', upstream, values_wide)
        row_dot = jnp.transpose(lax.optimization_barrier(jnp.sum(upstream * out_block, axis=-1)), (1, 2, 0))[..., None]
        grad_scores = (probability * (grad_probs - row_dot) * HEAD ** (-0.5)).astype(jnp.bfloat16).astype(jnp.float32)
        query_grads.append(jnp.einsum('kgqt,tkd->qkgd', grad_scores, keys_wide))
        key_sum = key_sum + jnp.einsum('kgqt,qkgd->tkd', grad_scores, query_block)
        value_sum = value_sum + jnp.einsum('kgqt,qkgd->tkd', weights_b, upstream)
    return (jnp.concatenate(query_grads, axis=0), key_sum, value_sum)

def one_sequence(hidden_row, cot_row, segment_row, position_row, weights):
    attention_gain, query_weight, key_weight, value_weight, output_weight, feed_gain, gate_weight, up_weight, down_weight = weights
    length = hidden_row.shape[0]
    group_size = HEADS // KV_HEADS
    input_wide = hidden_row.astype(jnp.float32)
    normed_one, unit_one, inverse_one = rms_forward(input_wide, attention_gain)
    normed_one_b = normed_one.astype(jnp.bfloat16)
    cosine, sine_part = rope_angles(position_row)
    query_b = rotate(matmul(normed_one_b, query_weight).reshape(length, HEADS, HEAD), cosine, sine_part, 1.0).astype(jnp.bfloat16)
    key_b = rotate(matmul(normed_one_b, key_weight).reshape(length, KV_HEADS, HEAD), cosine, sine_part, 1.0).astype(jnp.bfloat16)
    value_b = matmul(normed_one_b, value_weight).reshape(length, KV_HEADS, HEAD).astype(jnp.bfloat16)
    query_four = query_b.reshape(length, KV_HEADS, group_size, HEAD)
    attended_four, totals = attention_forward(query_four, key_b, value_b, segment_row)
    attended_b = attended_four.reshape(length, HEADS * HEAD)
    residual = input_wide + matmul(attended_b, output_weight)
    normed_two, unit_two, inverse_two = rms_forward(residual, feed_gain)
    normed_two_b = normed_two.astype(jnp.bfloat16)
    gate_pre = matmul(normed_two_b, gate_weight)
    up_pre = matmul(normed_two_b, up_weight)
    sigmoid_gate = jax.nn.sigmoid(gate_pre)
    hidden_b = (gate_pre * sigmoid_gate * up_pre).astype(jnp.bfloat16)
    layer_row = (residual + matmul(hidden_b, down_weight)).astype(jnp.bfloat16)
    cot_wide = cot_row.astype(jnp.float32)
    grad_hidden = matmul(cot_row, down_weight.T)
    grad_gate_pre = (grad_hidden * up_pre * sigmoid_gate * (1.0 + gate_pre * (1.0 - sigmoid_gate))).astype(jnp.bfloat16)
    grad_up_pre = (grad_hidden * gate_pre * sigmoid_gate).astype(jnp.bfloat16)
    grad_down = matmul(hidden_b.T, cot_row)
    grad_gate = matmul(normed_two_b.T, grad_gate_pre)
    grad_up = matmul(normed_two_b.T, grad_up_pre)
    grad_normed_two = matmul(grad_gate_pre, gate_weight.T) + matmul(grad_up_pre, up_weight.T)
    back_two, gain_two_term = rms_backward(grad_normed_two, unit_two, inverse_two, feed_gain)
    grad_residual = cot_wide + back_two
    grad_residual_b = grad_residual.astype(jnp.bfloat16)
    grad_output = matmul(attended_b.T, grad_residual_b)
    grad_attended = matmul(grad_residual_b, output_weight.T).astype(jnp.bfloat16)
    upstream_four = grad_attended.reshape(length, KV_HEADS, group_size, HEAD)
    grad_q, grad_k, grad_v = attention_backward(query_four, key_b, value_b, segment_row, attended_four, upstream_four, totals)
    grad_query_b = rotate(grad_q.reshape(length, HEADS, HEAD), cosine, sine_part, -1.0).astype(jnp.bfloat16).reshape(length, HEADS * HEAD)
    grad_key_b = rotate(grad_k, cosine, sine_part, -1.0).astype(jnp.bfloat16).reshape(length, KV_HEADS * HEAD)
    grad_value_b = grad_v.astype(jnp.bfloat16).reshape(length, KV_HEADS * HEAD)
    grad_query = matmul(normed_one_b.T, grad_query_b)
    grad_key = matmul(normed_one_b.T, grad_key_b)
    grad_value = matmul(normed_one_b.T, grad_value_b)
    grad_normed_one = matmul(grad_query_b, query_weight.T) + matmul(grad_key_b, key_weight.T) + matmul(grad_value_b, value_weight.T)
    back_one, gain_one_term = rms_backward(grad_normed_one, unit_one, inverse_one, attention_gain)
    grad_row = grad_residual + back_one
    grads = (gain_one_term, grad_query, grad_key, grad_value, grad_output, gain_two_term, grad_gate, grad_up, grad_down)
    return (layer_row, grad_row, grads)

def reference(hidden_in, cotangent, segment_ids, positions, attention_gain, query_weight, key_weight, value_weight, output_weight, feed_gain, gate_weight, up_weight, down_weight):
    weights = (attention_gain, query_weight, key_weight, value_weight, output_weight, feed_gain, gate_weight, up_weight, down_weight)

    def step_one(carry, inputs):
        hidden_row, cot_row, segment_row, position_row = inputs
        layer_row, grad_row, grads = one_sequence(hidden_row, cot_row, segment_row, position_row, weights)
        carry = jax.tree.map(lambda total, term: total + term, carry, grads)
        return (carry, (layer_row, grad_row))
    zeros = tuple((jnp.zeros(weight.shape, jnp.float32) for weight in weights))
    totals, outputs = lax.scan(step_one, zeros, (hidden_in, cotangent, segment_ids, positions))
    layer_out, grad_input = outputs
    return (layer_out, grad_input, totals[0], totals[1], totals[2], totals[3], totals[4], totals[5], totals[6], totals[7], totals[8])
```

```python
import math

import jax
import jax.numpy as jnp
from jax import lax
from jax.sharding import PartitionSpec as P

HEAD = 64
NORM_EPS = 1e-05
ROPE_BASE = 500000.0
MASKED = -1e30
BF = jnp.bfloat16
F32 = jnp.float32


def contract(left, right, left_dim, right_dim):
    return lax.dot_general(
        left, right, (((left_dim,), (right_dim,)), ((), ())), preferred_element_type=F32
    )


def rms_forward(values, gain):
    inverse = lax.rsqrt(jnp.mean(values * values, axis=-1, keepdims=True) + NORM_EPS)
    normed = values * inverse
    return (normed * gain, normed, inverse)


def rms_backward(upstream, normed, inverse, gain):
    scaled = upstream * gain
    result = inverse * (scaled - normed * jnp.mean(scaled * normed, axis=-1, keepdims=True))
    return (result, jnp.sum(upstream * normed, axis=0))


def rope_angles(positions):
    inverse_freq = ROPE_BASE ** (-(jnp.arange(HEAD // 2, dtype=F32) * 2.0 / HEAD))
    angles = positions.astype(F32)[:, None] * inverse_freq[None, :]
    return (jnp.cos(angles)[:, None, :], jnp.sin(angles)[:, None, :])


def rotate(tensor, cosine, sine_part, turn):
    rows, cols = tensor.shape
    heads = tensor.reshape(rows, cols // HEAD, HEAD)
    first = heads[..., : HEAD // 2]
    second = heads[..., HEAD // 2 :]
    return jnp.concatenate(
        [first * cosine - turn * second * sine_part, second * cosine + turn * first * sine_part],
        axis=-1,
    ).reshape(rows, cols)


def xor_bits(size):
    bits = []
    bit = 1
    while bit < size:
        bits.append(bit)
        bit *= 2
    assert bit == size
    return bits


def xor_offsets(size):
    offsets = [0]
    for bit in reversed(xor_bits(size)):
        offsets = offsets + [o ^ bit for o in offsets]
    return offsets


def swap(value, axis, offset):
    size = lax.axis_size(axis)
    return lax.ppermute(value, axis, [(i, i ^ offset) for i in range(size)])


def shift(value, steps):
    size = lax.axis_size("shard")
    return lax.ppermute(value, "shard", [(i, (i + steps) % size) for i in range(size)])


def xor_gather(value, axis, dim):
    for bit in reversed(xor_bits(lax.axis_size(axis))):
        value = jnp.concatenate([value, swap(value, axis, bit)], axis=dim)
    return value


def xor_scatter(value, axis):
    for bit in xor_bits(lax.axis_size(axis)):
        half = value.shape[0] // 2
        other = swap(value[half:].astype(BF), axis, bit)
        value = value[:half].astype(F32) + other.astype(F32)
    return value


def ring_gather(value):
    pieces = [value]
    for _ in range(lax.axis_size("shard") - 1):
        pieces.append(shift(pieces[-1], 1))
    return pieces


def ring_scatter(terms):
    count = len(terms)
    total = terms[1 % count]
    for r in range(2, count + 1):
        total = shift(total.astype(BF), 1).astype(F32) + terms[r % count]
    return total


def turn_blocks(value, dim):
    count = lax.axis_size("shard")
    me = lax.axis_index("shard")
    size = value.shape[dim] // count
    return jnp.concatenate(
        [
            lax.dynamic_slice_in_dim(value, ((me - b) % count) * size, size, dim)
            for b in range(count)
        ],
        axis=dim,
    )


def own_part(value, axis, dim, offset=0):
    count = lax.axis_size(axis)
    size = value.shape[dim] // count
    return lax.dynamic_slice_in_dim(value, (lax.axis_index(axis) ^ offset) * size, size, dim)


def in_true_order(pieces, axis):
    count = lax.axis_size(axis)
    me = lax.axis_index(axis)
    offsets = xor_offsets(count)
    ordered = []
    for index in range(count):
        chosen = pieces[0]
        for j in range(1, count):
            chosen = jnp.where((me ^ offsets[j]) == index, pieces[j], chosen)
        ordered.append(chosen)
    return ordered


def gain_total(vector):
    for axis in ("tensor", "context"):
        for bit in xor_bits(lax.axis_size(axis)):
            vector = vector + swap(vector, axis, bit)
    count = lax.axis_size("shard")
    me = lax.axis_index("shard")
    size = vector.shape[0] // count
    total = lax.dynamic_slice_in_dim(vector, me * size, size, 0)
    for r in range(1, count):
        total = total + shift(lax.dynamic_slice_in_dim(vector, ((me + r) % count) * size, size, 0), r)
    return total


def local(
    hidden_in,
    cotangent,
    segment_ids,
    positions,
    attention_gain,
    query_weight,
    key_weight,
    value_weight,
    output_weight,
    feed_gain,
    gate_weight,
    up_weight,
    down_weight,
):
    n = lax.axis_size("shard")
    m = lax.axis_size("context")
    k = lax.axis_size("tensor")
    ctx = lax.axis_index("context")
    ten = lax.axis_index("tensor")
    t_offsets = xor_offsets(k)
    c_offsets = xor_offsets(m)
    _, rows, width = hidden_in.shape
    share = rows // k
    scale = 1.0 / math.sqrt(HEAD)
    block = width // n

    def rows_rel(value, dim=0, base=0):
        return jnp.concatenate(
            [
                lax.dynamic_slice_in_dim(value, base + (ten ^ o) * share, share, dim)
                for o in t_offsets
            ],
            axis=dim,
        )

    gains = jnp.stack([attention_gain, feed_gain])
    gains = turn_blocks(
        jnp.concatenate([gains] + [shift(gains, r) for r in range(1, n)], axis=1), 1
    ).astype(F32)
    gain_one, gain_two = gains[0], gains[1]

    kv_part = key_weight.shape[1] // HEAD // m
    q_cols = query_weight.shape[1] // m
    kv_cols = kv_part * HEAD
    part_cols = q_cols + 2 * kv_cols

    def qkv_part(offset):
        return jnp.concatenate(
            [own_part(w, "context", 1, offset) for w in (query_weight, key_weight, value_weight)],
            axis=1,
        )

    qkv_ring = ring_gather(qkv_part(0))
    qkv_w = [jnp.concatenate([qkv_part(o) for o in c_offsets], axis=1)] + [
        xor_gather(piece, "context", 1) for piece in qkv_ring[1:]
    ]
    out_ring = ring_gather(own_part(output_weight, "context", 0))
    out_w = [jnp.concatenate([own_part(output_weight, "context", 0, o) for o in c_offsets])] + [
        xor_gather(piece, "context", 0) for piece in out_ring[1:]
    ]

    unit_part = gate_weight.shape[1] // n // m

    def in_weight(weight):
        parts = weight.reshape(block, n, m, unit_part)
        mine = lax.dynamic_index_in_dim(parts, ctx, 2, keepdims=False).transpose(1, 0, 2)
        mine = lax.all_to_all(mine, "shard", 0, 0, tiled=True).reshape(width, unit_part)
        return xor_gather(mine, "context", 1)

    def out_weight(weight):
        parts = weight.reshape(n, m, unit_part, block)
        mine = lax.dynamic_index_in_dim(parts, ctx, 1, keepdims=False)
        mine = lax.all_to_all(mine, "shard", 0, 0, tiled=True)
        mine = mine.transpose(1, 0, 2).reshape(unit_part, width)
        return xor_gather(mine, "context", 0)

    gate_w = in_weight(gate_weight)
    up_w = in_weight(up_weight)
    down_w = out_weight(down_weight)

    hidden_rows = hidden_in[0]
    x_wide = rows_rel(hidden_rows).astype(F32)
    normed_one, unit_one, inverse_one = rms_forward(x_wide, gain_one)
    normed_one_b = turn_blocks(normed_one.astype(BF), 1)
    cosine, sine_part = rope_angles(rows_rel(positions[0]))
    qkv = sum(
        contract(normed_one_b[:, r * block : (r + 1) * block], qkv_w[r], 1, 0) for r in range(n)
    )
    query_parts = []
    key_parts = []
    value_parts = []
    for j in range(m):
        low = j * part_cols
        query_parts.append(qkv[:, low : low + q_cols])
        key_parts.append(qkv[:, low + q_cols : low + q_cols + kv_cols])
        value_parts.append(qkv[:, low + q_cols + kv_cols : low + part_cols])
    query_b = rotate(jnp.concatenate(query_parts, axis=1), cosine, sine_part, 1.0).astype(BF)
    key_b = rotate(jnp.concatenate(key_parts, axis=1), cosine, sine_part, 1.0).astype(BF)
    value_b = jnp.concatenate(value_parts, axis=1).astype(BF)

    def parts_for(value, offset):
        cols = value.shape[1] // m
        pieces = [value[:, j * cols : (j + 1) * cols] for j in range(m)]
        return jnp.concatenate([pieces[c_offsets.index(o ^ offset)] for o in c_offsets], axis=1)

    own_kv = jnp.concatenate([key_b, value_b], axis=1)
    kv_blocks = [own_kv] + [
        swap(jnp.concatenate([parts_for(key_b, o), parts_for(value_b, o)], axis=1), "context", o)
        for o in c_offsets[1:]
    ]
    kv_all = jnp.concatenate(kv_blocks, axis=0)
    kv_width = key_b.shape[1]
    key_all, value_all = kv_all[:, :kv_width], kv_all[:, kv_width:]

    segments = [
        rows_rel(segment_ids[0], 0, (ctx ^ o) * rows) for o in c_offsets
    ]
    iota = jnp.arange(share, dtype=jnp.int32)
    places = [
        jnp.concatenate([(ctx ^ o) * rows + (ten ^ q) * share + iota for q in t_offsets])
        for o in c_offsets
    ]
    allowed = (places[0][:, None] >= jnp.concatenate(places)[None, :]) & (
        segments[0][:, None] == jnp.concatenate(segments)[None, :]
    )

    kv_heads = kv_width // HEAD
    group = query_b.shape[1] // kv_width
    group_cols = group * HEAD
    head_outputs = []
    head_totals = []
    for h in range(kv_heads):
        key_block = key_all[:, h * HEAD : (h + 1) * HEAD]
        value_block = value_all[:, h * HEAD : (h + 1) * HEAD]
        query_block = query_b[:, h * group_cols : (h + 1) * group_cols].reshape(rows, group, HEAD)
        scores = jnp.einsum("qgd,td->gqt", query_block, key_block, preferred_element_type=F32)
        scores = jnp.where(allowed[None], scores * scale, MASKED)
        log_total = jnp.log(jnp.sum(jnp.exp(scores), axis=-1, keepdims=True))
        weights_b = jnp.exp(scores - log_total).astype(BF)
        attended = jnp.einsum("gqt,td->qgd", weights_b, value_block, preferred_element_type=F32)
        head_outputs.append(attended.astype(BF).reshape(rows, group_cols))
        head_totals.append(log_total)
    attended_b = jnp.concatenate(head_outputs, axis=1)

    attention_part = jnp.concatenate([contract(attended_b, w, 1, 0) for w in out_w], axis=1)
    attention_sum = xor_scatter(attention_part, "tensor")
    x_own = own_part(hidden_rows, "tensor", 0).astype(F32)
    residual = x_own + turn_blocks(attention_sum, 1)
    normed_two, unit_two, inverse_two = rms_forward(residual, gain_two)
    normed_two_b = normed_two.astype(BF)

    cot_rows = rows_rel(cotangent[0])
    cot_ring = ring_gather(cot_rows[:share])
    cots = [cot_rows] + [xor_gather(piece, "tensor", 0) for piece in cot_ring[1:]]
    acts = [xor_gather(piece, "tensor", 0) for piece in ring_gather(normed_two_b)]
    hiddens = []
    gate_backs = []
    up_backs = []
    feed_terms = []
    back_terms = []
    for r in range(n):
        gate_pre = contract(acts[r], gate_w, 1, 0)
        up_pre = contract(acts[r], up_w, 1, 0)
        sig = jax.nn.sigmoid(gate_pre)
        hidden_b = (gate_pre * sig * up_pre).astype(BF)
        grad_hidden = contract(cots[r], down_w, 1, 1)
        gate_back = (grad_hidden * up_pre * sig * (1.0 + gate_pre * (1.0 - sig))).astype(BF)
        up_back = (grad_hidden * gate_pre * sig).astype(BF)
        back_terms.append(
            xor_scatter(contract(gate_back, gate_w, 1, 1) + contract(up_back, up_w, 1, 1), "tensor")
        )
        feed_terms.append(xor_scatter(contract(hidden_b, down_w, 1, 0), "tensor"))
        hiddens.append(hidden_b)
        gate_backs.append(gate_back)
        up_backs.append(up_back)
    grad_normed_two = ring_scatter(back_terms)
    layer_out = (residual + ring_scatter(feed_terms)).astype(BF)[None]

    all_acts = jnp.concatenate(acts)
    all_cots = jnp.concatenate(cots)
    grad_gate = contract(all_acts, jnp.concatenate(gate_backs), 0, 0)
    grad_up = contract(all_acts, jnp.concatenate(up_backs), 0, 0)
    grad_down = contract(jnp.concatenate(hiddens), all_cots, 0, 0)

    def sum_parts(value, dim):
        for bit in xor_bits(m):
            half = value.shape[dim] // 2
            kept = lax.slice_in_dim(value, 0, half, axis=dim)
            sent = lax.slice_in_dim(value, half, 2 * half, axis=dim)
            value = kept.astype(F32) + swap(sent.astype(BF), "context", bit).astype(F32)
        return value

    def all_parts(value):
        pieces = [value]
        for bit in reversed(xor_bits(m)):
            pieces = pieces + [swap(p, "context", bit) for p in pieces]
        return in_true_order(pieces, "context")

    def in_grad(total):
        part = sum_parts(total, 1).astype(BF).reshape(n, block, unit_part)
        part = lax.all_to_all(part, "shard", 0, 0, tiled=True)
        full = jnp.stack(all_parts(part), axis=2)
        return full.transpose(1, 0, 2, 3).reshape(block, n * m * unit_part).astype(F32)

    def out_grad(total):
        part = sum_parts(total, 0).astype(BF).reshape(unit_part, n, block).transpose(1, 0, 2)
        part = lax.all_to_all(part, "shard", 0, 0, tiled=True)
        full = jnp.stack(all_parts(part), axis=1)
        return full.reshape(n * m * unit_part, block).astype(F32)

    grad_gate_out = in_grad(grad_gate)
    grad_up_out = in_grad(grad_up)
    grad_down_out = out_grad(grad_down)

    cot_own = cot_rows[:share].astype(F32)
    back_two, gain_two_term = rms_backward(grad_normed_two, unit_two, inverse_two, gain_two)
    grad_residual = cot_own + back_two
    grad_feed_gain = gain_total(gain_two_term)

    grad_rows = xor_gather(turn_blocks(grad_residual.astype(BF), 1), "tensor", 0)
    grad_attended = sum(
        contract(grad_rows[:, r * block : (r + 1) * block], out_w[r], 1, 1) for r in range(n)
    ).astype(BF)
    grad_output = contract(attended_b, grad_rows, 0, 0)
    grad_output = sum_parts(grad_output, 0)
    grad_output = ring_scatter([grad_output[:, r * block : (r + 1) * block] for r in range(n)])
    grad_output_out = jnp.concatenate(all_parts(grad_output.astype(BF))).astype(F32)

    head_query = []
    head_key = []
    head_value = []
    for h in range(kv_heads):
        key_block = key_all[:, h * HEAD : (h + 1) * HEAD]
        value_block = value_all[:, h * HEAD : (h + 1) * HEAD]
        cols = slice(h * group_cols, (h + 1) * group_cols)
        query_block = query_b[:, cols].reshape(rows, group, HEAD)
        out_block = attended_b[:, cols].reshape(rows, group, HEAD)
        upstream = grad_attended[:, cols].reshape(rows, group, HEAD)
        scores = jnp.einsum("qgd,td->gqt", query_block, key_block, preferred_element_type=F32)
        scores = jnp.where(allowed[None], scores * scale, MASKED)
        probability = jnp.exp(scores - head_totals[h])
        weights_b = probability.astype(BF)
        grad_probs = jnp.einsum("qgd,td->gqt", upstream, value_block, preferred_element_type=F32)
        row_dot = jnp.transpose(jnp.sum(upstream.astype(F32) * out_block.astype(F32), axis=-1))
        grad_scores = (probability * (grad_probs - row_dot[:, :, None]) * scale).astype(BF)
        head_query.append(
            jnp.einsum("gqt,td->qgd", grad_scores, key_block, preferred_element_type=F32).reshape(
                rows, group_cols
            )
        )
        head_key.append(
            jnp.einsum("gqt,qgd->td", grad_scores, query_block, preferred_element_type=F32)
        )
        head_value.append(
            jnp.einsum("gqt,qgd->td", weights_b, upstream, preferred_element_type=F32)
        )
    query_grads = jnp.concatenate(head_query, axis=1)
    key_grads = jnp.concatenate(head_key, axis=1)
    value_grads = jnp.concatenate(head_value, axis=1)
    own_key, own_value = key_grads[:rows], value_grads[:rows]
    kv_sum = jnp.concatenate([own_key, own_value], axis=1)
    for j in range(1, m):
        o = c_offsets[j]
        sent = jnp.concatenate(
            [
                parts_for(key_grads[j * rows : (j + 1) * rows], o),
                parts_for(value_grads[j * rows : (j + 1) * rows], o),
            ],
            axis=1,
        )
        kv_sum = kv_sum + swap(sent.astype(BF), "context", o).astype(F32)
    grad_query_b = rotate(query_grads, cosine, sine_part, -1.0).astype(BF)
    grad_key_b = rotate(kv_sum[:, :kv_width], cosine, sine_part, -1.0).astype(BF)
    grad_value_b = kv_sum[:, kv_width:].astype(BF)
    grad_qkv = jnp.concatenate(
        [
            piece
            for j in range(m)
            for piece in (
                grad_query_b[:, j * q_cols : (j + 1) * q_cols],
                grad_key_b[:, j * kv_cols : (j + 1) * kv_cols],
                grad_value_b[:, j * kv_cols : (j + 1) * kv_cols],
            )
        ],
        axis=1,
    )
    weight_terms = [
        sum_parts(contract(normed_one_b[:, r * block : (r + 1) * block], grad_qkv, 0, 0), 1)
        for r in range(n)
    ]
    qkv_total = jnp.stack(all_parts(ring_scatter(weight_terms).astype(BF)), axis=1).astype(F32)
    grad_query_out = qkv_total[:, :, :q_cols].reshape(block, m * q_cols)
    grad_key_out = qkv_total[:, :, q_cols : q_cols + kv_cols].reshape(block, m * kv_cols)
    grad_value_out = qkv_total[:, :, q_cols + kv_cols :].reshape(block, m * kv_cols)

    attention_back = jnp.concatenate([contract(grad_qkv, w, 1, 1) for w in qkv_w], axis=1)
    grad_normed_one = turn_blocks(xor_scatter(attention_back, "tensor"), 1)
    back_one, gain_one_term = rms_backward(
        grad_normed_one, unit_one[:share], inverse_one[:share], gain_one
    )
    grad_input = (grad_residual + back_one)[None]
    grad_attention_gain = gain_total(gain_one_term)
    return (
        layer_out,
        grad_input,
        grad_attention_gain,
        grad_query_out,
        grad_key_out,
        grad_value_out,
        grad_output_out,
        grad_feed_gain,
        grad_gate_out,
        grad_up_out,
        grad_down_out,
    )


def solution(mesh):
    placed = (
        P("shard", "context", None),
        P("shard", "context", None),
        P("shard", None),
        P("shard", "context"),
        P("shard"),
        P("shard", "tensor"),
        P("shard", "tensor"),
        P("shard", "tensor"),
        P("tensor", "shard"),
        P("shard"),
        P("shard", "tensor"),
        P("shard", "tensor"),
        P("tensor", "shard"),
    )
    return jax.shard_map(
        local,
        mesh=mesh,
        in_specs=placed,
        out_specs=(
            P("shard", ("context", "tensor"), None),
            P("shard", ("context", "tensor"), None),
            P("shard"),
            P("shard", "tensor"),
            P("shard", "tensor"),
            P("shard", "tensor"),
            P("tensor", "shard"),
            P("shard"),
            P("shard", "tensor"),
            P("shard", "tensor"),
            P("tensor", "shard"),
        ),
        check_vma=False,
    )
```

```python
import math

import jax
import jax.numpy as jnp
from jax import lax
from jax.experimental import pallas as pl
from jax.experimental.pallas import tpu as pltpu
from jax.sharding import PartitionSpec as P


HEAD = 64
NORM_EPS = 1e-05
ROPE_BASE = 500000.0
MASKED = -1e30
BF = jnp.bfloat16
SH, CX, TN = "shard", "context", "tensor"
F32 = jnp.float32


def contract(left, right, left_dim, right_dim):
    return lax.dot_general(
        left, right, (((left_dim,), (right_dim,)), ((), ())), preferred_element_type=F32
    )


def xor_bits(size):
    bits = []
    bit = 1
    while bit < size:
        bits.append(bit)
        bit *= 2
    assert bit == size
    return bits


def xor_offsets(size):
    offsets = [0]
    for bit in reversed(xor_bits(size)):
        offsets = offsets + [o ^ bit for o in offsets]
    return offsets


def swap(value, axis, offset):
    size = lax.axis_size(axis)
    return lax.ppermute(value, axis, [(i, i ^ offset) for i in range(size)])


def shift(value, steps):
    size = lax.axis_size(SH)
    return lax.ppermute(value, SH, [(i, (i + steps) % size) for i in range(size)])


def after(value, *others):
    return lax.optimization_barrier((value,) + others)[0]


def gather_direct(value):
    return [value] + [swap(value, CX, o) for o in xor_offsets(lax.axis_size(CX))[1:]]


def turn_blocks(value, dim):
    count = lax.axis_size(SH)
    me = lax.axis_index(SH)
    size = value.shape[dim] // count
    return jnp.concatenate(
        [
            lax.dynamic_slice_in_dim(value, ((me - b) % count) * size, size, dim)
            for b in range(count)
        ],
        axis=dim,
    )


def own_part(value, axis, dim, offset=0):
    count = lax.axis_size(axis)
    size = value.shape[dim] // count
    return lax.dynamic_slice_in_dim(value, (lax.axis_index(axis) ^ offset) * size, size, dim)


def gain_total(vectors):
    for axis in (TN, CX):
        for bit in xor_bits(lax.axis_size(axis)):
            vectors = vectors + swap(vectors, axis, bit)
    count = lax.axis_size(SH)
    me = lax.axis_index(SH)
    size = vectors.shape[1] // count
    total = lax.dynamic_slice_in_dim(vectors, me * size, size, 1)
    for r in range(1, count):
        part = lax.dynamic_slice_in_dim(vectors, ((me + r) % count) * size, size, 1)
        total = total + shift(part, r)
    return total


def whole(count):
    return [pl.BlockSpec(memory_space=pl.ANY)] * count


def params():
    return pltpu.CompilerParams(vmem_limit_bytes=56 * 1024 * 1024)


def mlp_kernel(first, r, n, k, m, refs):
    place, refs = refs[0], refs[1:]
    heads = k if r else 2 * k
    acts, cots, weights = refs[:k], refs[k:heads], refs[heads : heads + n * m]
    kept = 2 + 2 * m
    rest = refs[heads + n * m + (0 if first else kept) :]
    all_acts, all_cots, all_hid, all_back = rest[0], rest[1], rest[2 : 2 + m], rest[2 + m : kept]
    low, high = rest[kept : kept + 2]
    a_v, c_v, gu_v, d_v, hid_v, back_v, low_v, high_v, in_sem, out_sem = rest[kept + 2 :]
    rows, width = a_v.shape
    share, block = rows // k, width // n
    units = d_v.shape[2]
    here = pl.ds(r * rows, rows)
    gets = []

    def get(source, target):
        copy = pltpu.make_async_copy(source, target, in_sem.at[len(gets)])
        copy.start()
        gets.append(copy)
        return copy

    top, bottom = pl.ds(0, share), pl.ds(share, share)
    a_get = [get(acts[j].at[top], a_v.at[pl.ds(j * share, share)]) for j in range(k)]
    gu_get = [
        [get(weights[i * m + j].at[pl.ds(0, block)], gu_v.at[j, at(place, 1 + i, block)]) for i in range(n)]
        for j in range(m)
    ]
    c_get = [
        get(acts[j].at[bottom] if r else cots[j], c_v.at[pl.ds(j * share, share)]) for j in range(k)
    ]
    d_get = [
        [get(weights[i * m + j].at[pl.ds(block, units)], d_v.at[j, i]) for i in range(n)]
        for j in range(m)
    ]
    puts = []

    def put(source, target):
        copy = pltpu.make_async_copy(source, target, out_sem.at[len(puts)])
        copy.start()
        puts.append(copy)

    for copy in a_get:
        copy.wait()
    put(a_v, all_acts.at[here])
    pres = []
    for j in range(m):
        for copy in gu_get[j]:
            copy.wait()
        pres.append(jnp.dot(a_v[...], gu_v[j], preferred_element_type=F32))
    for copy in c_get:
        copy.wait()
    put(c_v, all_cots.at[here])
    for j in range(m):
        for copy in d_get[j]:
            copy.wait()
        gate, up = pres[j][:, :units], pres[j][:, units:]
        sig = 1.0 / (1.0 + jnp.exp(-gate))
        act = gate * sig
        hid_v[j] = (act * up).astype(BF)
        grad = 0.0
        for i in range(n):
            grad += contract(c_v[:, at(place, 1 + i, block)], d_v[j, i], 1, 1)
        gate_back = grad * up * sig * (1.0 + gate * (1.0 - sig))
        back_v[j, :, :units] = gate_back.astype(BF)
        back_v[j, :, units:] = (grad * act).astype(BF)
        put(hid_v.at[j], all_hid[j].at[here])
        put(back_v.at[j], all_back[j].at[here])
    half = rows // 2

    def grad_in(part):
        total = 0.0
        for j in range(m):
            total += contract(back_v[j, part, :], gu_v[j], 1, 1)
        return total

    high_v[...] = grad_in(slice(half, rows)).astype(BF)
    put(high_v, high)
    low_v[...] = grad_in(slice(0, half))
    put(low_v, low)
    for copy in puts:
        copy.wait()


def mlp_chunk(r, n, m, place, acts, cots, weights, carried):
    k = len(acts)
    width = acts[0].shape[1]
    share = acts[0].shape[0] // (2 if r else 1)
    rows, block = share * k, width // n
    units = weights[0].shape[1] // 2
    first = carried is None
    total = n * rows
    sizes = [width] * 2 + [units] * m + [2 * units] * m
    big = [jax.ShapeDtypeStruct((total, cols), BF) for cols in sizes]
    outs = big + [
        jax.ShapeDtypeStruct((rows // 2, width), F32),
        jax.ShapeDtypeStruct((rows // 2, width), BF),
    ]
    operands = [place] + list(acts) + list(cots) + list(weights)
    aliases = {}
    if not first:
        aliases = {len(operands) + i: i for i in range(len(big))}
        operands = operands + list(carried)
    res = pl.pallas_call(
        lambda *refs: mlp_kernel(first, r, n, k, m, refs),
        out_shape=outs,
        in_specs=[pl.BlockSpec(memory_space=pltpu.SMEM)] + whole(len(operands) - 1),
        out_specs=whole(len(outs)),
        input_output_aliases=aliases,
        scratch_shapes=[
            pltpu.VMEM((rows, width), BF),
            pltpu.VMEM((rows, width), BF),
            pltpu.VMEM((m, width, 2 * units), BF),
            pltpu.VMEM((m, n, units, block), BF),
            pltpu.VMEM((m, rows, units), BF),
            pltpu.VMEM((m, rows, 2 * units), BF),
            pltpu.VMEM((rows // 2, width), F32),
            pltpu.VMEM((rows // 2, width), BF),
            pltpu.SemaphoreType.DMA((2 * k + 2 * n * m,)),
            pltpu.SemaphoreType.DMA((4 + 2 * m,)),
        ],
        compiler_params=params(),
        name="mc",
    )(*operands)
    return res[: len(big)], res[-2], res[-1]


def feed_kernel(n, m, block, place, *refs):
    hid, weights, low, high = refs[:m], refs[m : m + n * m], refs[m + n * m], refs[m + n * m + 1]
    rows = hid[0].shape[1]
    half = rows // 2
    for i in range(n):
        total = 0.0
        for j in range(m):
            total += jnp.dot(hid[j][0], weights[i * m + j][block:, :], preferred_element_type=F32)
        low[0, :, at(place, 1 + i, block)] = total[:half].astype(BF)
        high[0, :, at(place, 1 + i, block)] = total[half:].astype(BF)


def feed_out(place, hid, weights, rows, n):
    m = len(hid)
    units = hid[0].shape[1]
    block = weights[0].shape[0] - units
    width = n * block
    out = jax.ShapeDtypeStruct((n, rows // 2, width), BF)
    return pl.pallas_call(
        lambda *refs: feed_kernel(n, m, block, *refs),
        grid=(n,),
        out_shape=[out, out],
        in_specs=[pl.BlockSpec(memory_space=pltpu.SMEM)]
        + [pl.BlockSpec((1, rows, units), lambda i: (i, 0, 0)) for _ in hid]
        + [pl.BlockSpec(w.shape, lambda i: (0, 0)) for w in weights],
        out_specs=[pl.BlockSpec((1, rows // 2, width), lambda i: (i, 0, 0))] * 2,
        compiler_params=params(),
        name="fo",
    )(place, *[h.reshape(n, rows, units) for h in hid], *weights)


def feed_add_kernel(place, low, received, kept, sent):
    half = kept.shape[0]
    total = low[0].astype(F32) + received[0].astype(F32)
    kept[...] = total[:half]
    sent[...] = total[half:].astype(BF)


def feed_add(place, low, received):
    n, rows, width = low.shape
    half = rows // 2
    part = pl.BlockSpec((None, half, width), lambda i: (i, 0, 0))
    full = pl.BlockSpec((1, rows, width), lambda i: (i, 0, 0))
    return pl.pallas_call(
        feed_add_kernel,
        grid=(n,),
        out_shape=[jax.ShapeDtypeStruct((n, half, width), t) for t in (F32, BF)],
        in_specs=[pl.BlockSpec(memory_space=pltpu.SMEM), full, full],
        out_specs=[part, part],
        compiler_params=params(),
        name="fa",
    )(place, low, received)


def spread_kernel(n, m, place, gate, up, down, *outs):
    me = place[0]
    rows, cols = gate.shape
    units = cols // n // m
    offsets = xor_offsets(m)

    def fill(out, source, want):
        low = pl.multiple_of(source * (m * units), m * units)
        for value, col in ((gate, 0), (up, units)):
            both = value[:, pl.ds(low, m * units)]
            chosen = both[:, :units]
            for index in range(1, m):
                chosen = jnp.where(want == index, both[:, index * units : (index + 1) * units], chosen)
            out[:rows, col : col + units] = chosen
        row = pl.multiple_of((source * m + want) * units, units)
        out[rows:, :] = down[pl.ds(row, units), :]

    for j in range(m):
        fill(outs[j], place[1], me ^ offsets[j])
    for r in range(1, n):
        fill(outs[m + r - 1], place[1 + n - r], me)


def spread_units(place, gate, up, down, n, m):
    rows, cols = gate.shape
    units = cols // n // m
    assert down.shape[1] == rows == 2 * units
    vmem = pl.BlockSpec(memory_space=pltpu.VMEM)
    return pl.pallas_call(
        lambda *refs: spread_kernel(n, m, *refs),
        out_shape=[jax.ShapeDtypeStruct((rows + units, 2 * units), BF)] * (m + n - 1),
        in_specs=[pl.BlockSpec(memory_space=pltpu.SMEM)] + [vmem] * 3,
        out_specs=[vmem] * (m + n - 1),
        compiler_params=params(),
        name="su",
    )(place, gate, up, down)


def unit_grad_kernel(count, place, acts, cots, hid, back, *outs):
    block = acts.shape[1]
    top = contract(acts[...], back[...], 0, 0)
    bottom = contract(hid[...], cots[...], 0, 0)
    for i in range(count):

        @pl.when(pl.program_id(0) == i)
        def _(out=outs[i]):
            out[:block, :] = top.astype(out.dtype)
            out[block:, :] = bottom.astype(out.dtype)


def unit_grads(place, acts, cots, hid, back, dtype, n, first, count):
    rows, width = acts.shape
    block, units = width // n, hid.shape[1]
    out = jax.ShapeDtypeStruct((block + units, 2 * units), dtype)
    cols = pl.BlockSpec((rows, block), lambda i, place: (0, place[1 + (first + i) % n]))

    def all_of(shape):
        return pl.BlockSpec(shape, lambda i, place: (0, 0))

    return list(
        pl.pallas_call(
            lambda *refs: unit_grad_kernel(count, *refs),
            out_shape=[out] * count,
            grid_spec=pltpu.PrefetchScalarGridSpec(
                num_scalar_prefetch=1,
                grid=(count,),
                in_specs=[cols, cols, all_of(hid.shape), all_of(back.shape)],
                out_specs=[all_of(out.shape)] * count,
            ),
            compiler_params=params(),
        )(place, acts, cots, hid, back)
    )


def join_kernel(r, n, m, first, place, *refs):
    pieces = refs[:m]
    gate, up, down, gate_v, up_v, down_v, sems = refs[m + (0 if first else 3) :]
    units = pieces[0].shape[1] // 2
    block = pieces[0].shape[0] - units
    me = place[0]
    offsets = xor_offsets(m)
    for index in range(m):
        chosen = pieces[0][...].astype(F32)
        for j in range(1, m):
            chosen = jnp.where((me ^ offsets[j]) == index, pieces[j][...].astype(F32), chosen)
        gate_v[:, index * units : (index + 1) * units] = chosen[:block, :units]
        up_v[:, index * units : (index + 1) * units] = chosen[:block, units:]
        down_v[index * units : (index + 1) * units, :] = chosen[block:, :]
    there = at(place, 1 + (n - r) % n, m * units)
    copies = [
        pltpu.make_async_copy(gate_v, gate.at[:, there], sems.at[0]),
        pltpu.make_async_copy(up_v, up.at[:, there], sems.at[1]),
        pltpu.make_async_copy(down_v, down.at[there], sems.at[2]),
    ]
    for copy in copies:
        copy.start()
    for copy in copies:
        copy.wait()


def join_units(place, r, n, pieces, carried):
    m = len(pieces)
    units = pieces[0].shape[1] // 2
    block = pieces[0].shape[0] - units
    total = n * m * units
    vmem = pl.BlockSpec(memory_space=pltpu.VMEM)
    operands = [place, *pieces] + (list(carried) if carried else [])
    return pl.pallas_call(
        lambda *refs: join_kernel(r, n, m, not carried, *refs),
        out_shape=[shaped((block, total), F32)] * 2 + [shaped((total, block), F32)],
        in_specs=[pl.BlockSpec(memory_space=pltpu.SMEM)] + [vmem] * m + whole(3 if carried else 0),
        out_specs=whole(3),
        input_output_aliases={1 + m + i: i for i in range(3)} if carried else {},
        scratch_shapes=[
            pltpu.VMEM((block, m * units), F32),
            pltpu.VMEM((block, m * units), F32),
            pltpu.VMEM((m * units, block), F32),
            pltpu.SemaphoreType.DMA((3,)),
        ],
        compiler_params=params(),
        name="ju",
    )(*operands)


def pick_kernel(m, offsets, place, *refs):
    weights, outs = refs[:3], refs[3:]
    me = place[0]
    for j in range(m):
        low = 0
        for w in weights:
            cols = w.shape[1] // m
            chosen = w[:, :cols]
            for index in range(1, m):
                chosen = jnp.where((me ^ offsets[j]) == index, w[:, index * cols : (index + 1) * cols], chosen)
            outs[j][:, low : low + cols] = chosen
            low += cols


def pick_parts(weights, m):
    rows = weights[0].shape[0]
    cols = sum(w.shape[1] for w in weights) // m
    me = lax.axis_index(CX).astype(jnp.int32).reshape(1)
    offsets = xor_offsets(m)
    return pl.pallas_call(
        lambda *refs: pick_kernel(m, offsets, *refs),
        out_shape=[jax.ShapeDtypeStruct((rows, cols), BF)] * m,
        in_specs=[pl.BlockSpec(memory_space=pltpu.SMEM)] + [pl.BlockSpec(memory_space=pltpu.VMEM)] * 3,
        out_specs=[pl.BlockSpec(memory_space=pltpu.VMEM)] * m,
        compiler_params=params(),
        name="pp",
    )(me, *weights)


def join_rows_kernel(m, offsets, place, *refs):
    pieces, out = refs[:m], refs[m]
    n, units, _ = pieces[0].shape
    me = place[0]
    for b in range(n):
        for index in range(m):
            chosen = pieces[0][b].astype(F32)
            for j in range(1, m):
                chosen = jnp.where((me ^ offsets[j]) == index, pieces[j][b].astype(F32), chosen)
            low = (b * m + index) * units
            out[low : low + units, :] = chosen


def join_rows(pieces):
    m = len(pieces)
    n, units, cols = pieces[0].shape
    me = lax.axis_index(CX).astype(jnp.int32).reshape(1)
    offsets = xor_offsets(m)
    return pl.pallas_call(
        lambda *refs: join_rows_kernel(m, offsets, *refs),
        out_shape=jax.ShapeDtypeStruct((n * m * units, cols), F32),
        in_specs=[pl.BlockSpec(memory_space=pltpu.SMEM)] + [pl.BlockSpec(memory_space=pltpu.VMEM)] * m,
        out_specs=pl.BlockSpec(memory_space=pltpu.VMEM),
        compiler_params=params(),
        name="jr",
    )(me, *pieces)


def scalars(*values):
    return jnp.stack([jnp.asarray(v, jnp.int32) for v in values])


def call(kernel, outs, operands, scratch=()):
    vmem = pl.BlockSpec(memory_space=pltpu.VMEM)
    return pl.pallas_call(
        kernel,
        out_shape=outs,
        in_specs=[pl.BlockSpec(memory_space=pltpu.SMEM)] + [vmem] * (len(operands) - 1),
        out_specs=jax.tree.map(lambda _: vmem, outs),
        scratch_shapes=scratch,
        compiler_params=params(),
    )(*operands)


def shaped(shape, dtype):
    return jax.ShapeDtypeStruct(shape, dtype)


def at(base, index, size):
    return pl.ds(pl.multiple_of(base[index] * size, size), size)


def norm_kernel(n, k, place, hidden, gains, out):
    rows = hidden.shape[0]
    share = rows // k
    gain = gains[0:1, :].astype(F32)
    for j in range(k):
        x = hidden[at(place, 1 + n + j, share), :].astype(F32)
        inverse = lax.rsqrt(jnp.mean(x * x, axis=-1, keepdims=True) + NORM_EPS)
        out[j * share : (j + 1) * share, :] = (x * inverse * gain).astype(BF)


def turn_heads(u, cosine, sine, turn):
    width = u.shape[1]
    half = HEAD // 2
    place = lax.broadcasted_iota(jnp.int32, u.shape, 1) % HEAD
    other = jnp.where(place < half, pltpu.roll(u, width - half, 1), pltpu.roll(u, half, 1))
    reps = width // cosine.shape[1]
    cos_all = jnp.concatenate([cosine] * reps, axis=1) if reps > 1 else cosine
    sin_all = jnp.concatenate([sine] * reps, axis=1) if reps > 1 else sine
    return u * cos_all + turn * other * sin_all


def qkv_kernel(n, m, q_cols, kv_cols, place, normed, cosine, sine, *refs):
    weights, query, kv_own, kv_sends = refs[: n * m], refs[n * m], refs[n * m + 1], refs[n * m + 2 :]
    block = normed.shape[1] // n
    totals = []
    for j in range(m):
        total = 0.0
        for r in range(n):
            x = normed[:, at(place, 1 + r, block)]
            total += jnp.dot(x, weights[r * m + j][...], preferred_element_type=F32)
        totals.append(total)
    cos, sin = cosine[...], sine[...]
    for j in range(m):
        turned = turn_heads(totals[j][:, :q_cols], cos, sin, 1.0)
        query[:, j * q_cols : (j + 1) * q_cols] = turned.astype(BF)
    keys = jnp.concatenate([t[:, q_cols : q_cols + kv_cols] for t in totals], axis=1)
    keys = turn_heads(keys, cos, sin, 1.0).astype(BF)
    keys = [keys[:, j * kv_cols : (j + 1) * kv_cols] for j in range(m)]
    values = [t[:, q_cols + kv_cols :].astype(BF) for t in totals]
    offsets = xor_offsets(m)
    for o, out in zip(offsets, (kv_own,) + tuple(kv_sends)):
        order = [offsets.index(p ^ o) for p in offsets]
        out[...] = jnp.concatenate([keys[j] for j in order] + [values[j] for j in order], axis=1)


def mask_bias(n, k, rows, place, seg_row, seg_col, order):
    share = rows // k
    me = place[0]
    blocks = []
    q_seg = []
    q_place = []
    step = lax.broadcasted_iota(jnp.int32, (share, 1), 0)
    lane = lax.broadcasted_iota(jnp.int32, (1, share), 1)
    for j in range(k):
        base = pl.multiple_of(me * rows + place[1 + n + j] * share, share)
        q_seg.append(seg_col[pl.ds(base, share), :])
        q_place.append(step + base)
    q_seg = jnp.concatenate(q_seg, axis=0)
    q_place = jnp.concatenate(q_place, axis=0)
    for o in order:
        for j in range(k):
            base = pl.multiple_of((me ^ o) * rows + place[1 + n + j] * share, share)
            k_seg = seg_row[:, pl.ds(base, share)]
            seen = (q_place >= lane + base) & (q_seg == k_seg)
            blocks.append(jnp.where(seen, 0.0, MASKED))
    return jnp.concatenate(blocks, axis=1)


def attend_kernel(n, m, k, place, query, seg_row, seg_col, kv_own, *refs):
    kv, attended, totals = (kv_own,) + refs[: m - 1], refs[m - 1], refs[m]
    bias_v, keys_v = refs[m + 1], refs[m + 2]
    rows, q_width = query.shape
    kv_width = kv_own.shape[1] // 2
    heads, kv_heads = q_width // HEAD, kv_width // HEAD
    group = heads // kv_heads
    bias_v[...] = mask_bias(n, k, rows, place, seg_row, seg_col, xor_offsets(m))
    for i in range(m):
        keys_v[i * rows : (i + 1) * rows, :] = kv[i][...]
    lanes = lax.broadcasted_iota(jnp.int32, totals.shape, 1)
    kept = jnp.zeros(totals.shape, F32)
    for h in range(heads):
        g = h // group
        q = query[:, h * HEAD : (h + 1) * HEAD] * (1.0 / math.sqrt(HEAD))
        scores = contract(q.astype(BF), keys_v[:, g * HEAD : (g + 1) * HEAD], 1, 1) + bias_v[...]
        log_total = jnp.log(jnp.sum(jnp.exp(scores), axis=1, keepdims=True))
        prob = jnp.exp(scores - log_total).astype(BF)
        value = keys_v[:, kv_width + g * HEAD : kv_width + (g + 1) * HEAD]
        out = jnp.dot(prob, value, preferred_element_type=F32)
        attended[:, h * HEAD : (h + 1) * HEAD] = out.astype(BF)
        kept = jnp.where(lanes == h, log_total, kept)
    totals[...] = kept


def out_weight(m, place, out_w, firsts, others, r, j):
    part = out_w.shape[0] // m
    if r == 0:
        row = pl.multiple_of((place[0] ^ xor_offsets(m)[j]) * part, part)
        return out_w[pl.ds(row, part), :]
    if j == 0:
        return firsts[r - 1][...]
    return others[j - 1][r - 1]


def out_kernel(n, m, place, attended, out_w, *refs):
    firsts, others = refs[: n - 1], refs[n - 1 : n + m - 2]
    low, high = refs[n + m - 2 :]
    rows, cols = attended.shape
    part, half = cols // m, rows // 2
    block = out_w.shape[1]
    for r in range(n):
        total = 0.0
        for j in range(m):
            w = out_weight(m, place, out_w, firsts, others, r, j)
            total += jnp.dot(attended[:, j * part : (j + 1) * part], w, preferred_element_type=F32)
        low[:, at(place, 1 + r, block)] = total[:half]
        high[:, at(place, 1 + r, block)] = total[half:].astype(BF)


def residual_kernel(place, kept, received, hidden, gains, cot, residual, normed, stream):
    share = kept.shape[0]
    total = hidden[...].astype(F32) + (kept[...] + received[...].astype(F32))
    inverse = lax.rsqrt(jnp.mean(total * total, axis=-1, keepdims=True) + NORM_EPS)
    residual[...] = total
    result = (total * inverse * gains[1:2, :].astype(F32)).astype(BF)
    normed[...] = result
    stream[:share, :] = result
    stream[share:, :] = cot[...]


def norm_back(upstream, values, gain):
    inverse = lax.rsqrt(jnp.mean(values * values, axis=-1, keepdims=True) + NORM_EPS)
    unit = values * inverse
    scaled = upstream * gain
    result = inverse * (scaled - unit * jnp.mean(scaled * unit, axis=-1, keepdims=True))
    return result, jnp.sum(upstream * unit, axis=0, keepdims=True)


def feed_back_kernel(place, kept, received, residual, gains, cot, *refs):
    moved, grad, grad_b, gain_term = refs[:-3], *refs[-3:]
    upstream = kept[...] + received[...].astype(F32)
    for part in moved:
        upstream += part[...].astype(F32)
    result, term = norm_back(upstream, residual[...], gains[1:2, :].astype(F32))
    result += cot[...].astype(F32)
    grad[...] = result
    grad_b[...] = result.astype(BF)
    gain_term[...] = term


def input_back_kernel(place, kept, received, hidden, gains, grad_residual, out, gain_term):
    x = hidden[...].astype(F32)
    upstream = kept[...] + received[...].astype(F32)
    result, term = norm_back(upstream, x, gains[0:1, :].astype(F32))
    out[...] = grad_residual[...] + result
    gain_term[...] = term


def out_back_kernel(n, m, k, place, out_w, *refs):
    grads, refs = refs[:k], refs[k:]
    firsts, others = refs[: n - 1], refs[n - 1 : n + m - 2]
    attended_grad, grads_v = refs[n + m - 2 :]
    share, width = grads[0].shape
    block = width // n
    part = attended_grad.shape[1] // m
    for i in range(k):
        grads_v[i * share : (i + 1) * share, :] = grads[i][...]
    for j in range(m):
        total = 0.0
        for r in range(n):
            w = out_weight(m, place, out_w, firsts, others, r, j)
            total += contract(grads_v[:, at(place, 1 + r, block)], w, 1, 1)
        attended_grad[:, j * part : (j + 1) * part] = total.astype(BF)


def out_grad_kernel(n, m, place, attended, grads, *outs):
    part, block = attended.shape[1] // m, grads.shape[1] // n
    for j in reversed(range(m)):
        for r in range(n):
            total = contract(attended[:, j * part : (j + 1) * part], grads[:, at(place, 1 + r, block)], 0, 0)
            outs[r][j * part : (j + 1) * part, :] = total.astype(outs[r].dtype)


def attend_back_kernel(n, m, k, place, query, seg_row, seg_col, attended, upstream, totals, kv_own, *refs):
    kv, refs = (kv_own,) + refs[: m - 1], refs[m - 1 :]
    query_grad, kv_grad, kv_sends = refs[0], refs[1], refs[2 : 1 + m]
    bias_v, keys_v, grads_v = refs[1 + m :]
    rows, q_width = query.shape
    kv_width = kv_own.shape[1] // 2
    heads, kv_heads = q_width // HEAD, kv_width // HEAD
    group = heads // kv_heads
    scale = 1.0 / math.sqrt(HEAD)
    offsets = xor_offsets(m)
    bias_v[...] = mask_bias(n, k, rows, place, seg_row, seg_col, offsets)
    for i in range(m):
        keys_v[i * rows : (i + 1) * rows, :] = kv[i][...]
    for g in range(kv_heads):
        key = keys_v[:, g * HEAD : (g + 1) * HEAD]
        value = keys_v[:, kv_width + g * HEAD : kv_width + (g + 1) * HEAD]
        key_sum, value_sum = 0.0, 0.0
        for h in range(g * group, (g + 1) * group):
            cols = slice(h * HEAD, (h + 1) * HEAD)
            q, up = query[:, cols], upstream[:, cols]
            row_dot = jnp.sum(up.astype(F32) * attended[:, cols].astype(F32), axis=1, keepdims=True)
            scores = contract((q * scale).astype(BF), key, 1, 1) + bias_v[...]
            prob = jnp.exp(scores - totals[:, h : h + 1])
            grad_prob = contract(up, value, 1, 1)
            grad_scores = (prob * ((grad_prob - row_dot) * scale)).astype(BF)
            query_grad[:, cols] = jnp.dot(grad_scores, key, preferred_element_type=F32)
            key_sum += contract(grad_scores, q, 0, 0)
            value_sum += contract(prob.astype(BF), up, 0, 0)
        grads_v[:, g * HEAD : (g + 1) * HEAD] = key_sum
        grads_v[:, kv_width + g * HEAD : kv_width + (g + 1) * HEAD] = value_sum
    kv_grad[...] = grads_v[:rows, :]
    cols = kv_width // m
    for i in range(1, m):
        here = grads_v[i * rows : (i + 1) * rows, :]
        order = [offsets.index(p ^ offsets[i]) for p in offsets]
        pieces = [here[:, low + j * cols : low + (j + 1) * cols] for low in (0, kv_width) for j in order]
        kv_sends[i - 1][...] = jnp.concatenate(pieces, axis=1).astype(BF)


def join_grads_kernel(m, q_cols, kv_cols, place, query_grad, kv_grad, cosine, sine, *refs):
    received, outs = refs[: m - 1], refs[m - 1 :]
    kv_width = m * kv_cols
    cos, sin = cosine[...], sine[...]
    total = kv_grad[...]
    for piece in received:
        total += piece[...].astype(F32)
    keys = turn_heads(total[:, :kv_width], cos, sin, -1.0).astype(BF)
    values = total[:, kv_width:].astype(BF)
    for j in range(m):
        turned = turn_heads(query_grad[:, j * q_cols : (j + 1) * q_cols], cos, sin, -1.0)
        outs[j][:, :q_cols] = turned.astype(BF)
        outs[j][:, q_cols : q_cols + kv_cols] = keys[:, j * kv_cols : (j + 1) * kv_cols]
        outs[j][:, q_cols + kv_cols :] = values[:, j * kv_cols : (j + 1) * kv_cols]


def qkv_grad_kernel(n, place, normed, grads, *outs):
    block = normed.shape[1] // n
    for i in range(n):
        r = (1 + i) % n
        total = contract(normed[:, at(place, 1 + r, block)], grads[...], 0, 0)
        outs[r][...] = total.astype(outs[r].dtype)


def qkv_back_kernel(n, m, place, *refs):
    grads, weights, low, high = refs[:m], refs[m : m + n * m], refs[m + n * m], refs[m + n * m + 1]
    block = low.shape[1] // n
    half = low.shape[0]
    for r in range(n):
        total = 0.0
        for j in range(m):
            total += contract(grads[j][...], weights[r * m + j][...], 1, 1)
        low[:, at(place, 1 + r, block)] = total[:half]
        high[:, at(place, 1 + r, block)] = total[half:].astype(BF)


def qkv_join_kernel(m, offsets, q_cols, kv_cols, place, *refs):
    pieces, outs = refs[:m], refs[m:]
    me = place[0]
    for index in range(m):
        chosen = pieces[0][...].astype(F32)
        for j in range(1, m):
            chosen = jnp.where((me ^ offsets[j]) == index, pieces[j][...].astype(F32), chosen)
        low = 0
        for out, cols in zip(outs, (q_cols, kv_cols, kv_cols)):
            out[:, index * cols : (index + 1) * cols] = chosen[:, low : low + cols]
            low += cols


def local(
    hidden_in,
    cotangent,
    segment_ids,
    positions,
    attention_gain,
    query_weight,
    key_weight,
    value_weight,
    output_weight,
    feed_gain,
    gate_weight,
    up_weight,
    down_weight,
):
    n = lax.axis_size(SH)
    m = lax.axis_size(CX)
    k = lax.axis_size(TN)
    shard = lax.axis_index(SH)
    ctx = lax.axis_index(CX)
    ten = lax.axis_index(TN)
    t_offsets = xor_offsets(k)
    c_offsets = xor_offsets(m)
    _, rows, width = hidden_in.shape
    share = rows // k
    block = width // n
    place = scalars(ctx, *[(shard - r) % n for r in range(n)], *[ten ^ o for o in t_offsets])
    hidden, cot = hidden_in[0], cotangent[0]

    kv_part = key_weight.shape[1] // HEAD // m
    q_cols = query_weight.shape[1] // m
    kv_cols = kv_part * HEAD
    part_cols = q_cols + 2 * kv_cols
    qkv_parts = pick_parts((query_weight, key_weight, value_weight), m)
    qkv_w = [qkv_parts]
    piece = qkv_parts[0]
    for r in range(1, n):
        piece = shift(piece, 1)
        qkv_w.append(gather_direct(piece))
        if r == max(n - 2, 1):
            middle_piece = piece
    if n == 1:
        middle_piece = piece
    gains = after(jnp.stack([attention_gain, feed_gain]), qkv_parts[0])
    gains = turn_blocks(jnp.concatenate([gains] + [shift(gains, r) for r in range(1, n)], axis=1), 1)

    units_mine = spread_units(place, gate_weight, up_weight, down_weight, n, m)
    unit_w = [list(units_mine[:m])]
    cot_pieces = [
        lax.dynamic_slice_in_dim(cot, (ten ^ o) * share, share, 0) for o in t_offsets
    ]
    hidden_own = own_part(hidden, TN, 0)
    out_mine = own_part(output_weight, CX, 0)
    inverse_freq = ROPE_BASE ** (-(jnp.arange(HEAD // 2, dtype=F32) * 2.0 / HEAD))
    place_rows = jnp.concatenate(
        [lax.dynamic_slice_in_dim(positions[0], (ten ^ o) * share, share, 0) for o in t_offsets]
    )
    reps = m * kv_cols // (HEAD // 2)
    angles = place_rows.astype(F32)[:, None] * jnp.tile(inverse_freq, reps)[None, :]
    signs = jnp.tile(jnp.repeat(jnp.array([-1.0, 1.0], F32), HEAD // 2), reps // 2)
    cosine, sine = jnp.cos(angles), jnp.sin(angles) * signs[None, :]
    seg_row = segment_ids
    seg_col = segment_ids.reshape(-1, 1)

    normed_one = call(
        lambda *refs: norm_kernel(n, k, *refs), shaped((rows, width), BF), (place, hidden, gains)
    )
    out_mine = after(out_mine, middle_piece)
    out_firsts = []
    for r in range(1, n):
        out_firsts.append(shift(out_mine, r))
    flat_qkv = [w for parts in qkv_w for w in parts]
    query, kv_own, *kv_sends = call(
        lambda *refs: qkv_kernel(n, m, q_cols, kv_cols, *refs),
        [shaped((rows, m * q_cols), BF)] + [shaped((rows, 2 * m * kv_cols), BF)] * m,
        (place, normed_one, cosine, sine, *flat_qkv),
    )
    early_values = lax.optimization_barrier((kv_own, hidden_own, *cot_pieces, seg_col, middle_piece))
    kv_own, hidden_own, cot_pieces, seg_col = (
        early_values[0],
        early_values[1],
        list(early_values[2 : 2 + k]),
        early_values[2 + k],
    )
    kv_others = []
    for o, sent in zip(c_offsets[1:], kv_sends):
        kv_others.append(swap(sent, CX, o))
    out_stack = after(jnp.stack(out_firsts), kv_own)
    out_others = []
    for o in c_offsets[1:]:
        out_others.append(swap(out_stack, CX, o))
    units_sent = list(units_mine[m:])
    early = [r for r in range(1, n) if r != n // 2]
    moved = [None] * n
    for r in early:
        moved[r] = shift(units_sent[r - 1] if r == 1 else after(units_sent[r - 1], out_stack), r)
    wide = 2 * m * kv_cols
    attended, totals = call(
        lambda *refs: attend_kernel(n, m, k, *refs),
        [shaped((rows, m * q_cols), BF), shaped((rows, 128), F32)],
        (place, query, seg_row, seg_col, kv_own, *kv_others),
        [pltpu.VMEM((rows, m * rows), F32), pltpu.VMEM((m * rows, wide), BF)],
    )
    for r in range(1, n):
        if r not in early:
            moved[r] = shift(after(units_sent[r - 1], attended), r)
    low, high = call(
        lambda *refs: out_kernel(n, m, *refs),
        [shaped((rows // 2, width), F32), shaped((rows // 2, width), BF)],
        (place, attended, output_weight, *out_firsts, *out_others),
    )

    def scatter_open(low, high):
        bits = xor_bits(k)
        for i, bit in enumerate(bits):
            received = swap(high, TN, bit)
            if i + 1 < len(bits):
                total = low.astype(F32) + received.astype(F32)
                half = total.shape[-2] // 2
                low, high = total[..., :half, :], total[..., half:, :].astype(BF)
        return low, received

    kept, received = scatter_open(low, high)
    residual, normed_two, stream_own = call(
        residual_kernel,
        [shaped((share, width), F32), shaped((share, width), BF), shaped((2 * share, width), BF)],
        (place, kept, received, hidden_own, gains, cot_pieces[0]),
    )

    stream = [stream_own if n == 1 else after(stream_own, moved[n // 2])]
    for r in range(1, n):
        stream.append(shift(stream[-1], 1))
    for r in range(1, n):
        unit_w.append(gather_direct(after(moved[r], attended if r == 1 else normed_two)))
    flat_units = [w for parts in unit_w for w in parts]
    carried = None
    back_kept = []
    back_received = []
    for r in range(n):
        acts = [stream[r] if r else normed_two]
        for bit in reversed(xor_bits(k)):
            acts = acts + [swap(p, TN, bit) for p in acts]
        carried, low, high = mlp_chunk(
            r, n, m, place, acts, [] if r else cot_pieces, flat_units, carried
        )
        kept, received = scatter_open(low, high)
        back_kept.append(kept)
        back_received.append(received)
    back_moved = []
    for r in range(1, n):
        part = (back_kept[r] + back_received[r].astype(F32)).astype(BF)
        back_moved.append(shift(part, -r))
    grad_residual, grad_b, gain_two_term = call(
        feed_back_kernel,
        [shaped((share, width), F32), shaped((share, width), BF), shaped((1, width), F32)],
        (place, back_kept[0], back_received[0], residual, gains, cot_pieces[0], *back_moved),
    )
    all_acts, all_cots, all_hid, all_back = carried[0], carried[1], carried[2 : 2 + m], carried[2 + m :]

    def send_part(value, j):
        return swap(value.astype(BF), CX, c_offsets[j])

    unit_terms = [[] for _ in range(n)]
    for j in reversed(range(m)):
        half = n // 2 if j else n
        parts = [None] * n
        for first in range(1, n + 1, half):
            some = unit_grads(
                place, all_acts, all_cots, all_hid[j], all_back[j],
                BF if j else F32, n, first, half,
            )
            for i, value in enumerate(some):
                parts[(first + i) % n] = value
        for i in range(n):
            r = (1 + i) % n
            if j:
                if i >= n // 2:
                    parts[r] = after(parts[r], unit_terms[1 + i - n // 2][0])
                parts[r] = send_part(parts[r], j)
            unit_terms[r].append(parts[r])
    unit_totals = []
    for r in range(n):
        total = sum(t.astype(F32) for t in unit_terms[r]).astype(BF)
        if r:
            total = shift(total, -r)
        unit_totals.append(total)
    grads = [grad_b]
    for bit in reversed(xor_bits(k)):
        grads = grads + [swap(p, TN, bit) for p in grads]
    feed_low, feed_high = feed_out(place, [after(h, grad_b) for h in all_hid], flat_units, rows, n)
    attended_grad, all_grads = call(
        lambda *refs: out_back_kernel(n, m, k, *refs),
        [shaped((rows, m * q_cols), BF), shaped((rows, width), BF)],
        (place, output_weight, *grads, *out_firsts, *out_others),
    )
    query_grad, kv_grad, *kv_sends = call(
        lambda *refs: attend_back_kernel(n, m, k, *refs),
        [shaped((rows, m * q_cols), F32), shaped((rows, wide), F32)]
        + [shaped((rows, wide), BF)] * (m - 1),
        (place, query, seg_row, seg_col, attended, attended_grad, totals, kv_own, *kv_others),
        [
            pltpu.VMEM((rows, m * rows), F32),
            pltpu.VMEM((m * rows, wide), BF),
            pltpu.VMEM((m * rows, wide), F32),
        ],
    )
    kv_received = []
    for o, sent in zip(c_offsets[1:], kv_sends):
        kv_received.append(swap(sent, CX, o))
    out_grads = call(
        lambda *refs: out_grad_kernel(n, m, *refs),
        [shaped((m * q_cols, block), BF if r == 1 % n else F32) for r in range(n)],
        (place, attended, after(all_grads, kv_grad)),
    )
    feed_bits = xor_bits(k)
    for i, bit in enumerate(feed_bits):
        if i + 1 == len(feed_bits):
            feed_high = after(feed_high, kv_grad)
        feed_received = swap(feed_high, TN, bit)
        if i + 1 < len(feed_bits):
            feed_low, feed_high = feed_add(place, after(feed_low, kv_grad), feed_received)
    feed_sum = feed_low.astype(F32) + feed_received.astype(F32)
    total = feed_sum[1 % n]
    for r in range(2, n + 1):
        moved_on = shift(total.astype(BF), 1)
        total = moved_on.astype(F32) + feed_sum[r % n]
    layer_out = (residual + total).astype(BF)[None]

    qkv_grads = call(
        lambda *refs: join_grads_kernel(m, q_cols, kv_cols, *refs),
        [shaped((rows, part_cols), BF)] * m,
        (place, query_grad, kv_grad, cosine, sine, *kv_received),
    )
    terms = [[] for _ in range(n)]
    for j in reversed(range(m)):
        parts = list(call(
            lambda *refs: qkv_grad_kernel(n, *refs),
            [shaped((block, part_cols), BF if j else F32)] * n,
            (place, normed_one, qkv_grads[j]),
        ))
        for i in range(n):
            r = (1 + i) % n
            if j:
                parts[r] = send_part(parts[r], j)
            terms[r].append(parts[r])
    total = after(out_grads[1 % n], terms[0][-1])
    for r in range(2, n + 1):
        total = shift(total.astype(BF), 1)
        total = total.astype(F32) + out_grads[r % n]
    parts = [total[j * q_cols : (j + 1) * q_cols] for j in range(m)]
    sums = list(parts)
    for o in c_offsets[1:]:
        order = [c_offsets.index(p ^ o) for p in c_offsets]
        got = swap(jnp.concatenate([parts[i] for i in order]).astype(BF), CX, o)
        sums = [s + got[j * q_cols : (j + 1) * q_cols].astype(F32) for j, s in enumerate(sums)]
    grad_output_out = join_rows([s[None] for s in sums])
    unit_parts = []
    for r in range(n):
        unit_parts.append(gather_direct(after(unit_totals[r], terms[0][-1] if r else kv_grad)))
    low, high = call(
        lambda *refs: qkv_back_kernel(n, m, *refs),
        [shaped((rows // 2, width), F32), shaped((rows // 2, width), BF)],
        (place, *qkv_grads, *flat_qkv),
    )
    kept, received = scatter_open(low, high)
    total = None
    for i in range(n):
        r = (1 + i) % n
        term = sum(t.astype(F32) for t in terms[r])
        if r:
            term = shift(term.astype(BF), -r).astype(F32)
        total = term if total is None else total + term
    qkv_parts_out = gather_direct(total.astype(BF))
    grad_query_out, grad_key_out, grad_value_out = call(
        lambda *refs: qkv_join_kernel(m, c_offsets, q_cols, kv_cols, *refs),
        [shaped((block, m * cols), F32) for cols in (q_cols, kv_cols, kv_cols)],
        (place, *qkv_parts_out),
    )
    grad_input, gain_one_term = call(
        input_back_kernel,
        [shaped((share, width), F32), shaped((1, width), F32)],
        (place, kept, received, hidden_own, gains, grad_residual),
    )
    gain_one, gain_two = gain_total(jnp.concatenate([gain_one_term, gain_two_term]))
    joined = None
    for r in range(n):
        joined = join_units(place, r, n, unit_parts[r], joined)
    grad_gate_out, grad_up_out, grad_down_out = joined
    return (
        layer_out,
        grad_input[None],
        gain_one,
        grad_query_out,
        grad_key_out,
        grad_value_out,
        grad_output_out,
        gain_two,
        grad_gate_out,
        grad_up_out,
        grad_down_out,
    )


def solution(mesh):
    placed = (
        P(SH, CX, None),
        P(SH, CX, None),
        P(SH, None),
        P(SH, CX),
        P(SH),
        P(SH, TN),
        P(SH, TN),
        P(SH, TN),
        P(TN, SH),
        P(SH),
        P(SH, TN),
        P(SH, TN),
        P(TN, SH),
    )

    return jax.shard_map(
        local,
        mesh=mesh,
        in_specs=placed,
        out_specs=(
            P(SH, (CX, TN), None),
            P(SH, (CX, TN), None),
            P(SH),
            P(SH, TN),
            P(SH, TN),
            P(SH, TN),
            P(TN, SH),
            P(SH),
            P(SH, TN),
            P(SH, TN),
            P(TN, SH),
        ),
        check_vma=False,
    )
```

```python
import math

import jax
import jax.numpy as jnp
from jax import lax
from jax.experimental import pallas as pl
from jax.experimental.pallas import tpu as pltpu
from jax.sharding import PartitionSpec as P


HEAD = 64
NORM_EPS = 1e-05
ROPE_BASE = 500000.0
MASKED = -1e30
BF = jnp.bfloat16
SH, CX, TN = "shard", "context", "tensor"
F32 = jnp.float32


def contract(left, right, left_dim, right_dim):
    return lax.dot_general(
        left, right, (((left_dim,), (right_dim,)), ((), ())), preferred_element_type=F32
    )


def xor_bits(size):
    bits = []
    bit = 1
    while bit < size:
        bits.append(bit)
        bit *= 2
    assert bit == size
    return bits


def xor_offsets(size):
    offsets = [0]
    for bit in reversed(xor_bits(size)):
        offsets = offsets + [o ^ bit for o in offsets]
    return offsets


def swap(value, axis, offset):
    size = lax.axis_size(axis)
    return lax.ppermute(value, axis, [(i, i ^ offset) for i in range(size)])


def shift(value, steps):
    size = lax.axis_size(SH)
    return lax.ppermute(value, SH, [(i, (i + steps) % size) for i in range(size)])


def after(value, *others):
    return lax.optimization_barrier((value,) + others)[0]


def gather_direct(value):
    return [value] + [swap(value, CX, o) for o in xor_offsets(lax.axis_size(CX))[1:]]


def shard_sum(terms):
    left = dict(enumerate(terms))
    for bit in xor_bits(len(terms)):
        kept = [o for o in left if not o & bit]
        sent = [left[o | bit].astype(BF) for o in kept]
        got = swap(jnp.stack(sent) if len(sent) > 1 else sent[0][None], SH, bit)
        left = {o: left[o].astype(F32) + got[i].astype(F32) for i, o in enumerate(kept)}
    return left[0]


def turn_blocks(value, dim):
    count = lax.axis_size(SH)
    me = lax.axis_index(SH)
    size = value.shape[dim] // count
    return jnp.concatenate(
        [
            lax.dynamic_slice_in_dim(value, ((me - b) % count) * size, size, dim)
            for b in range(count)
        ],
        axis=dim,
    )


def own_part(value, axis, dim, offset=0):
    count = lax.axis_size(axis)
    size = value.shape[dim] // count
    return lax.dynamic_slice_in_dim(value, (lax.axis_index(axis) ^ offset) * size, size, dim)


def gain_total(vectors):
    for axis in (TN, CX):
        for bit in xor_bits(lax.axis_size(axis)):
            vectors = vectors + swap(vectors, axis, bit)
    count = lax.axis_size(SH)
    me = lax.axis_index(SH)
    size = vectors.shape[1] // count
    total = lax.dynamic_slice_in_dim(vectors, me * size, size, 1)
    for r in range(1, count):
        part = lax.dynamic_slice_in_dim(vectors, ((me + r) % count) * size, size, 1)
        total = total + shift(part, r)
    return total


def whole(count):
    return [pl.BlockSpec(memory_space=pl.ANY)] * count


def params():
    return pltpu.CompilerParams(vmem_limit_bytes=56 * 1024 * 1024)


def mlp_kernel(first, r, n, k, m, refs):
    place, refs = refs[0], refs[1:]
    heads = k if r else 2 * k
    acts, cots, weights = refs[:k], refs[k:heads], refs[heads : heads + n * m]
    kept = 2 + 2 * m
    rest = refs[heads + n * m + (0 if first else kept) :]
    all_acts, all_cots, all_hid, all_back = rest[0], rest[1], rest[2 : 2 + m], rest[2 + m : kept]
    low, high = rest[kept : kept + 2]
    a_v, c_v, gu_v, d_v, hid_v, back_v, low_v, high_v, in_sem, out_sem = rest[kept + 2 :]
    rows, width = a_v.shape
    share, block = rows // k, width // n
    units = d_v.shape[2]
    here = pl.ds(r * rows, rows)
    gets = []

    def get(source, target):
        copy = pltpu.make_async_copy(source, target, in_sem.at[len(gets)])
        copy.start()
        gets.append(copy)
        return copy

    top, bottom = pl.ds(0, share), pl.ds(share, share)
    a_get = [get(acts[j].at[top], a_v.at[pl.ds(j * share, share)]) for j in range(k)]
    gu_get = [
        [get(weights[i * m + j].at[pl.ds(0, block)], gu_v.at[j, at(place, 1 + i, block)]) for i in range(n)]
        for j in range(m)
    ]
    c_get = [
        get(acts[j].at[bottom] if r else cots[j], c_v.at[pl.ds(j * share, share)]) for j in range(k)
    ]
    d_get = [
        [get(weights[i * m + j].at[pl.ds(block, units)], d_v.at[j, i]) for i in range(n)]
        for j in range(m)
    ]
    puts = []

    def put(source, target):
        copy = pltpu.make_async_copy(source, target, out_sem.at[len(puts)])
        copy.start()
        puts.append(copy)

    for copy in a_get:
        copy.wait()
    put(a_v, all_acts.at[here])
    pres = []
    for j in range(m):
        for copy in gu_get[j]:
            copy.wait()
        pres.append(jnp.dot(a_v[...], gu_v[j], preferred_element_type=F32))
    for copy in c_get:
        copy.wait()
    put(c_v, all_cots.at[here])
    for j in range(m):
        for copy in d_get[j]:
            copy.wait()
        gate, up = pres[j][:, :units], pres[j][:, units:]
        sig = 1.0 / (1.0 + jnp.exp(-gate))
        act = gate * sig
        hid_v[j] = (act * up).astype(BF)
        grad = 0.0
        for i in range(n):
            grad += contract(c_v[:, at(place, 1 + i, block)], d_v[j, i], 1, 1)
        gate_back = grad * up * sig * (1.0 + gate * (1.0 - sig))
        back_v[j, :, :units] = gate_back.astype(BF)
        back_v[j, :, units:] = (grad * act).astype(BF)
        put(hid_v.at[j], all_hid[j].at[here])
        put(back_v.at[j], all_back[j].at[here])
    half = rows // 2

    def grad_in(part):
        total = 0.0
        for j in range(m):
            total += contract(back_v[j, part, :], gu_v[j], 1, 1)
        return total

    high_v[...] = grad_in(slice(half, rows)).astype(BF)
    put(high_v, high)
    low_v[...] = grad_in(slice(0, half))
    put(low_v, low)
    for copy in puts:
        copy.wait()


def mlp_chunk(r, n, m, place, acts, cots, weights, carried):
    k = len(acts)
    width = acts[0].shape[1]
    share = acts[0].shape[0] // (2 if r else 1)
    rows, block = share * k, width // n
    units = weights[0].shape[1] // 2
    first = carried is None
    total = n * rows
    sizes = [width] * 2 + [units] * m + [2 * units] * m
    big = [jax.ShapeDtypeStruct((total, cols), BF) for cols in sizes]
    outs = big + [
        jax.ShapeDtypeStruct((rows // 2, width), F32),
        jax.ShapeDtypeStruct((rows // 2, width), BF),
    ]
    operands = [place] + list(acts) + list(cots) + list(weights)
    aliases = {}
    if not first:
        aliases = {len(operands) + i: i for i in range(len(big))}
        operands = operands + list(carried)
    res = pl.pallas_call(
        lambda *refs: mlp_kernel(first, r, n, k, m, refs),
        out_shape=outs,
        in_specs=[pl.BlockSpec(memory_space=pltpu.SMEM)] + whole(len(operands) - 1),
        out_specs=whole(len(outs)),
        input_output_aliases=aliases,
        scratch_shapes=[
            pltpu.VMEM((rows, width), BF),
            pltpu.VMEM((rows, width), BF),
            pltpu.VMEM((m, width, 2 * units), BF),
            pltpu.VMEM((m, n, units, block), BF),
            pltpu.VMEM((m, rows, units), BF),
            pltpu.VMEM((m, rows, 2 * units), BF),
            pltpu.VMEM((rows // 2, width), F32),
            pltpu.VMEM((rows // 2, width), BF),
            pltpu.SemaphoreType.DMA((2 * k + 2 * n * m,)),
            pltpu.SemaphoreType.DMA((4 + 2 * m,)),
        ],
        compiler_params=params(),
        name="mc",
    )(*operands)
    return res[: len(big)], res[-2], res[-1]


def feed_kernel(n, m, block, place, *refs):
    hid, weights, low, high = refs[:m], refs[m : m + n * m], refs[m + n * m], refs[m + n * m + 1]
    rows = hid[0].shape[1]
    half = rows // 2
    for i in range(n):
        total = 0.0
        for j in range(m):
            total += jnp.dot(hid[j][0], weights[i * m + j][block:, :], preferred_element_type=F32)
        low[0, :, at(place, 1 + i, block)] = total[:half].astype(BF)
        high[0, :, at(place, 1 + i, block)] = total[half:].astype(BF)


def feed_out(place, hid, weights, rows, n):
    m = len(hid)
    units = hid[0].shape[1]
    block = weights[0].shape[0] - units
    width = n * block
    out = jax.ShapeDtypeStruct((n, rows // 2, width), BF)
    return pl.pallas_call(
        lambda *refs: feed_kernel(n, m, block, *refs),
        grid=(n,),
        out_shape=[out, out],
        in_specs=[pl.BlockSpec(memory_space=pltpu.SMEM)]
        + [pl.BlockSpec((1, rows, units), lambda i: (i, 0, 0)) for _ in hid]
        + [pl.BlockSpec(w.shape, lambda i: (0, 0)) for w in weights],
        out_specs=[pl.BlockSpec((1, rows // 2, width), lambda i: (i, 0, 0))] * 2,
        compiler_params=params(),
        name="fo",
    )(place, *[h.reshape(n, rows, units) for h in hid], *weights)


def feed_add_kernel(place, low, received, kept, sent):
    half = kept.shape[0]
    total = low[0].astype(F32) + received[0].astype(F32)
    kept[...] = total[:half]
    sent[...] = total[half:].astype(BF)


def feed_add(places, low, received):
    n, rows, width = low.shape
    half = rows // 2
    part = pl.BlockSpec((None, half, width), lambda i, places: (i, 0, 0))
    full = pl.BlockSpec((1, rows, width), lambda i, places: (places[i], 0, 0))
    return pl.pallas_call(
        feed_add_kernel,
        out_shape=[jax.ShapeDtypeStruct((n, half, width), t) for t in (F32, BF)],
        grid_spec=pltpu.PrefetchScalarGridSpec(
            num_scalar_prefetch=1, grid=(n,), in_specs=[full, full], out_specs=[part, part]
        ),
        compiler_params=params(),
        name="fa",
    )(places, low, received)


def spread_kernel(n, m, place, gate, up, down, *outs):
    me = place[0]
    rows, cols = gate.shape
    units = cols // n // m
    offsets = xor_offsets(m)

    def fill(out, source, want):
        low = pl.multiple_of(source * (m * units), m * units)
        for value, col in ((gate, 0), (up, units)):
            both = value[:, pl.ds(low, m * units)]
            chosen = both[:, :units]
            for index in range(1, m):
                chosen = jnp.where(want == index, both[:, index * units : (index + 1) * units], chosen)
            out[:rows, col : col + units] = chosen
        row = pl.multiple_of((source * m + want) * units, units)
        out[rows:, :] = down[pl.ds(row, units), :]

    for j in range(m):
        fill(outs[j], place[1], me ^ offsets[j])
    for r in range(1, n):
        fill(outs[m + r - 1], place[1 + n - r], me)


def spread_units(place, gate, up, down, n, m):
    rows, cols = gate.shape
    units = cols // n // m
    assert down.shape[1] == rows == 2 * units
    vmem = pl.BlockSpec(memory_space=pltpu.VMEM)
    return pl.pallas_call(
        lambda *refs: spread_kernel(n, m, *refs),
        out_shape=[jax.ShapeDtypeStruct((rows + units, 2 * units), BF)] * (m + n - 1),
        in_specs=[pl.BlockSpec(memory_space=pltpu.SMEM)] + [vmem] * 3,
        out_specs=[vmem] * (m + n - 1),
        compiler_params=params(),
        name="su",
    )(place, gate, up, down)


def unit_grad_kernel(count, place, acts, cots, hid, back, *outs):
    block = acts.shape[1]
    top = contract(acts[...], back[...], 0, 0)
    bottom = contract(hid[...], cots[...], 0, 0)
    for i in range(count):

        @pl.when(pl.program_id(0) == i)
        def _(out=outs[i]):
            out[:block, :] = top.astype(out.dtype)
            out[block:, :] = bottom.astype(out.dtype)


def unit_grads(place, acts, cots, hid, back, dtype, n, first, count):
    rows, width = acts.shape
    block, units = width // n, hid.shape[1]
    out = jax.ShapeDtypeStruct((block + units, 2 * units), dtype)
    cols = pl.BlockSpec((rows, block), lambda i, place: (0, place[1 + (first + i) % n]))

    def all_of(shape):
        return pl.BlockSpec(shape, lambda i, place: (0, 0))

    return list(
        pl.pallas_call(
            lambda *refs: unit_grad_kernel(count, *refs),
            out_shape=[out] * count,
            grid_spec=pltpu.PrefetchScalarGridSpec(
                num_scalar_prefetch=1,
                grid=(count,),
                in_specs=[cols, cols, all_of(hid.shape), all_of(back.shape)],
                out_specs=[all_of(out.shape)] * count,
            ),
            compiler_params=params(),
        )(place, acts, cots, hid, back)
    )


def join_kernel(r, n, m, first, place, *refs):
    pieces = refs[:m]
    gate, up, down, gate_v, up_v, down_v, sems = refs[m + (0 if first else 3) :]
    units = pieces[0].shape[1] // 2
    block = pieces[0].shape[0] - units
    me = place[0]
    offsets = xor_offsets(m)
    for index in range(m):
        chosen = pieces[0][...].astype(F32)
        for j in range(1, m):
            chosen = jnp.where((me ^ offsets[j]) == index, pieces[j][...].astype(F32), chosen)
        gate_v[:, index * units : (index + 1) * units] = chosen[:block, :units]
        up_v[:, index * units : (index + 1) * units] = chosen[:block, units:]
        down_v[index * units : (index + 1) * units, :] = chosen[block:, :]
    there = at(place, 1 + (n - r) % n, m * units)
    copies = [
        pltpu.make_async_copy(gate_v, gate.at[:, there], sems.at[0]),
        pltpu.make_async_copy(up_v, up.at[:, there], sems.at[1]),
        pltpu.make_async_copy(down_v, down.at[there], sems.at[2]),
    ]
    for copy in copies:
        copy.start()
    for copy in copies:
        copy.wait()


def join_units(place, r, n, pieces, carried):
    m = len(pieces)
    units = pieces[0].shape[1] // 2
    block = pieces[0].shape[0] - units
    total = n * m * units
    vmem = pl.BlockSpec(memory_space=pltpu.VMEM)
    operands = [place, *pieces] + (list(carried) if carried else [])
    return pl.pallas_call(
        lambda *refs: join_kernel(r, n, m, not carried, *refs),
        out_shape=[shaped((block, total), F32)] * 2 + [shaped((total, block), F32)],
        in_specs=[pl.BlockSpec(memory_space=pltpu.SMEM)] + [vmem] * m + whole(3 if carried else 0),
        out_specs=whole(3),
        input_output_aliases={1 + m + i: i for i in range(3)} if carried else {},
        scratch_shapes=[
            pltpu.VMEM((block, m * units), F32),
            pltpu.VMEM((block, m * units), F32),
            pltpu.VMEM((m * units, block), F32),
            pltpu.SemaphoreType.DMA((3,)),
        ],
        compiler_params=params(),
        name="ju",
    )(*operands)


def pick_kernel(m, offsets, place, *refs):
    weights, outs = refs[:3], refs[3:]
    me = place[0]
    for j in range(m):
        low = 0
        for w in weights:
            cols = w.shape[1] // m
            chosen = w[:, :cols]
            for index in range(1, m):
                chosen = jnp.where((me ^ offsets[j]) == index, w[:, index * cols : (index + 1) * cols], chosen)
            outs[j][:, low : low + cols] = chosen
            low += cols


def pick_parts(weights, m):
    rows = weights[0].shape[0]
    cols = sum(w.shape[1] for w in weights) // m
    me = lax.axis_index(CX).astype(jnp.int32).reshape(1)
    offsets = xor_offsets(m)
    return pl.pallas_call(
        lambda *refs: pick_kernel(m, offsets, *refs),
        out_shape=[jax.ShapeDtypeStruct((rows, cols), BF)] * m,
        in_specs=[pl.BlockSpec(memory_space=pltpu.SMEM)] + [pl.BlockSpec(memory_space=pltpu.VMEM)] * 3,
        out_specs=[pl.BlockSpec(memory_space=pltpu.VMEM)] * m,
        compiler_params=params(),
        name="pp",
    )(me, *weights)


def join_rows_kernel(m, offsets, place, *refs):
    pieces, out = refs[:m], refs[m]
    n, units, _ = pieces[0].shape
    me = place[0]
    for b in range(n):
        for index in range(m):
            chosen = pieces[0][b].astype(F32)
            for j in range(1, m):
                chosen = jnp.where((me ^ offsets[j]) == index, pieces[j][b].astype(F32), chosen)
            low = (b * m + index) * units
            out[low : low + units, :] = chosen


def join_rows(pieces):
    m = len(pieces)
    n, units, cols = pieces[0].shape
    me = lax.axis_index(CX).astype(jnp.int32).reshape(1)
    offsets = xor_offsets(m)
    return pl.pallas_call(
        lambda *refs: join_rows_kernel(m, offsets, *refs),
        out_shape=jax.ShapeDtypeStruct((n * m * units, cols), F32),
        in_specs=[pl.BlockSpec(memory_space=pltpu.SMEM)] + [pl.BlockSpec(memory_space=pltpu.VMEM)] * m,
        out_specs=pl.BlockSpec(memory_space=pltpu.VMEM),
        compiler_params=params(),
        name="jr",
    )(me, *pieces)


def scalars(*values):
    return jnp.stack([jnp.asarray(v, jnp.int32) for v in values])


def call(kernel, outs, operands, scratch=()):
    vmem = pl.BlockSpec(memory_space=pltpu.VMEM)
    return pl.pallas_call(
        kernel,
        out_shape=outs,
        in_specs=[pl.BlockSpec(memory_space=pltpu.SMEM)] + [vmem] * (len(operands) - 1),
        out_specs=jax.tree.map(lambda _: vmem, outs),
        scratch_shapes=scratch,
        compiler_params=params(),
    )(*operands)


def shaped(shape, dtype):
    return jax.ShapeDtypeStruct(shape, dtype)


def at(base, index, size):
    return pl.ds(pl.multiple_of(base[index] * size, size), size)


def norm_kernel(n, k, place, hidden, gains, out):
    rows = hidden.shape[0]
    share = rows // k
    gain = gains[0:1, :].astype(F32)
    for j in range(k):
        x = hidden[at(place, 1 + n + j, share), :].astype(F32)
        inverse = lax.rsqrt(jnp.mean(x * x, axis=-1, keepdims=True) + NORM_EPS)
        out[j * share : (j + 1) * share, :] = (x * inverse * gain).astype(BF)


def turn_heads(u, cosine, sine, turn):
    width = u.shape[1]
    half = HEAD // 2
    place = lax.broadcasted_iota(jnp.int32, u.shape, 1) % HEAD
    other = jnp.where(place < half, pltpu.roll(u, width - half, 1), pltpu.roll(u, half, 1))
    reps = width // cosine.shape[1]
    cos_all = jnp.concatenate([cosine] * reps, axis=1) if reps > 1 else cosine
    sin_all = jnp.concatenate([sine] * reps, axis=1) if reps > 1 else sine
    return u * cos_all + turn * other * sin_all


def qkv_kernel(n, m, q_cols, kv_cols, place, normed, cosine, sine, *refs):
    weights, query, kv_own, kv_sends = refs[: n * m], refs[n * m], refs[n * m + 1], refs[n * m + 2 :]
    block = normed.shape[1] // n
    totals = []
    for j in range(m):
        total = 0.0
        for r in range(n):
            x = normed[:, at(place, 1 + r, block)]
            total += jnp.dot(x, weights[r * m + j][...], preferred_element_type=F32)
        totals.append(total)
    cos, sin = cosine[...], sine[...]
    for j in range(m):
        turned = turn_heads(totals[j][:, :q_cols], cos, sin, 1.0)
        query[:, j * q_cols : (j + 1) * q_cols] = turned.astype(BF)
    keys = jnp.concatenate([t[:, q_cols : q_cols + kv_cols] for t in totals], axis=1)
    keys = turn_heads(keys, cos, sin, 1.0).astype(BF)
    keys = [keys[:, j * kv_cols : (j + 1) * kv_cols] for j in range(m)]
    values = [t[:, q_cols + kv_cols :].astype(BF) for t in totals]
    offsets = xor_offsets(m)
    for o, out in zip(offsets, (kv_own,) + tuple(kv_sends)):
        order = [offsets.index(p ^ o) for p in offsets]
        out[...] = jnp.concatenate([keys[j] for j in order] + [values[j] for j in order], axis=1)


def mask_bias(n, k, rows, place, seg_row, seg_col, order):
    share = rows // k
    me = place[0]
    blocks = []
    q_seg = []
    q_place = []
    step = lax.broadcasted_iota(jnp.int32, (share, 1), 0)
    lane = lax.broadcasted_iota(jnp.int32, (1, share), 1)
    for j in range(k):
        base = pl.multiple_of(me * rows + place[1 + n + j] * share, share)
        q_seg.append(seg_col[pl.ds(base, share), :])
        q_place.append(step + base)
    q_seg = jnp.concatenate(q_seg, axis=0)
    q_place = jnp.concatenate(q_place, axis=0)
    for o in order:
        for j in range(k):
            base = pl.multiple_of((me ^ o) * rows + place[1 + n + j] * share, share)
            k_seg = seg_row[:, pl.ds(base, share)]
            seen = (q_place >= lane + base) & (q_seg == k_seg)
            blocks.append(jnp.where(seen, 0.0, MASKED))
    return jnp.concatenate(blocks, axis=1)


def attend_kernel(n, m, k, place, query, seg_row, seg_col, kv_own, *refs):
    kv, attended, totals = (kv_own,) + refs[: m - 1], refs[m - 1], refs[m]
    bias_v, keys_v = refs[m + 1], refs[m + 2]
    rows, q_width = query.shape
    kv_width = kv_own.shape[1] // 2
    heads, kv_heads = q_width // HEAD, kv_width // HEAD
    group = heads // kv_heads
    bias_v[...] = mask_bias(n, k, rows, place, seg_row, seg_col, xor_offsets(m))
    for i in range(m):
        keys_v[i * rows : (i + 1) * rows, :] = kv[i][...]
    lanes = lax.broadcasted_iota(jnp.int32, totals.shape, 1)
    kept = jnp.zeros(totals.shape, F32)
    for h in range(heads):
        g = h // group
        q = query[:, h * HEAD : (h + 1) * HEAD] * (1.0 / math.sqrt(HEAD))
        scores = contract(q.astype(BF), keys_v[:, g * HEAD : (g + 1) * HEAD], 1, 1) + bias_v[...]
        log_total = jnp.log(jnp.sum(jnp.exp(scores), axis=1, keepdims=True))
        prob = jnp.exp(scores - log_total).astype(BF)
        value = keys_v[:, kv_width + g * HEAD : kv_width + (g + 1) * HEAD]
        out = jnp.dot(prob, value, preferred_element_type=F32)
        attended[:, h * HEAD : (h + 1) * HEAD] = out.astype(BF)
        kept = jnp.where(lanes == h, log_total, kept)
    totals[...] = kept


def out_weight(m, place, out_w, firsts, others, r, j):
    part = out_w.shape[0] // m
    if r == 0:
        row = pl.multiple_of((place[0] ^ xor_offsets(m)[j]) * part, part)
        return out_w[pl.ds(row, part), :]
    if j == 0:
        return firsts[r - 1][...]
    return others[j - 1][r - 1]


def out_kernel(n, m, place, attended, out_w, *refs):
    firsts, others = refs[: n - 1], refs[n - 1 : n + m - 2]
    low, high = refs[n + m - 2 :]
    rows, cols = attended.shape
    part, half = cols // m, rows // 2
    block = out_w.shape[1]
    for r in range(n):
        total = 0.0
        for j in range(m):
            w = out_weight(m, place, out_w, firsts, others, r, j)
            total += jnp.dot(attended[:, j * part : (j + 1) * part], w, preferred_element_type=F32)
        low[:, at(place, 1 + r, block)] = total[:half]
        high[:, at(place, 1 + r, block)] = total[half:].astype(BF)


def residual_kernel(place, kept, received, hidden, gains, cot, residual, normed, stream):
    share = kept.shape[0]
    total = hidden[...].astype(F32) + (kept[...] + received[...].astype(F32))
    inverse = lax.rsqrt(jnp.mean(total * total, axis=-1, keepdims=True) + NORM_EPS)
    residual[...] = total
    result = (total * inverse * gains[1:2, :].astype(F32)).astype(BF)
    normed[...] = result
    stream[:share, :] = result
    stream[share:, :] = cot[...]


def norm_back(upstream, values, gain):
    inverse = lax.rsqrt(jnp.mean(values * values, axis=-1, keepdims=True) + NORM_EPS)
    unit = values * inverse
    scaled = upstream * gain
    result = inverse * (scaled - unit * jnp.mean(scaled * unit, axis=-1, keepdims=True))
    return result, jnp.sum(upstream * unit, axis=0, keepdims=True)


def feed_back_kernel(place, kept, received, residual, gains, cot, *refs):
    moved, grad, grad_b, gain_term = refs[:-3], *refs[-3:]
    upstream = kept[...] + received[...].astype(F32)
    for part in moved:
        upstream += part[...].astype(F32)
    result, term = norm_back(upstream, residual[...], gains[1:2, :].astype(F32))
    result += cot[...].astype(F32)
    grad[...] = result
    grad_b[...] = result.astype(BF)
    gain_term[...] = term


def input_back_kernel(place, kept, received, hidden, gains, grad_residual, out, gain_term):
    x = hidden[...].astype(F32)
    upstream = kept[...] + received[...].astype(F32)
    result, term = norm_back(upstream, x, gains[0:1, :].astype(F32))
    out[...] = grad_residual[...] + result
    gain_term[...] = term


def out_back_kernel(n, m, k, place, out_w, *refs):
    grads, refs = refs[:k], refs[k:]
    firsts, others = refs[: n - 1], refs[n - 1 : n + m - 2]
    attended_grad, grads_v = refs[n + m - 2 :]
    share, width = grads[0].shape
    block = width // n
    part = attended_grad.shape[1] // m
    for i in range(k):
        grads_v[i * share : (i + 1) * share, :] = grads[i][...]
    for j in range(m):
        total = 0.0
        for r in range(n):
            w = out_weight(m, place, out_w, firsts, others, r, j)
            total += contract(grads_v[:, at(place, 1 + r, block)], w, 1, 1)
        attended_grad[:, j * part : (j + 1) * part] = total.astype(BF)


def out_grad_kernel(n, m, k, place, attended, grads, *outs):
    part, block = attended.shape[1] // m, grads.shape[1] // n
    for j in reversed(range(m)):
        for r in range(n):
            total = contract(
                attended[:, j * part : (j + 1) * part], grads[:, at(place, 1 + n + k + r, block)], 0, 0
            )
            outs[r][j * part : (j + 1) * part, :] = total.astype(outs[r].dtype)


def attend_back_kernel(n, m, k, place, query, seg_row, seg_col, attended, upstream, totals, kv_own, *refs):
    kv, refs = (kv_own,) + refs[: m - 1], refs[m - 1 :]
    query_grad, kv_grad, kv_sends = refs[0], refs[1], refs[2 : 1 + m]
    bias_v, keys_v, grads_v = refs[1 + m :]
    rows, q_width = query.shape
    kv_width = kv_own.shape[1] // 2
    heads, kv_heads = q_width // HEAD, kv_width // HEAD
    group = heads // kv_heads
    scale = 1.0 / math.sqrt(HEAD)
    offsets = xor_offsets(m)
    bias_v[...] = mask_bias(n, k, rows, place, seg_row, seg_col, offsets)
    for i in range(m):
        keys_v[i * rows : (i + 1) * rows, :] = kv[i][...]
    for g in range(kv_heads):
        key = keys_v[:, g * HEAD : (g + 1) * HEAD]
        value = keys_v[:, kv_width + g * HEAD : kv_width + (g + 1) * HEAD]
        key_sum, value_sum = 0.0, 0.0
        for h in range(g * group, (g + 1) * group):
            cols = slice(h * HEAD, (h + 1) * HEAD)
            q, up = query[:, cols], upstream[:, cols]
            row_dot = jnp.sum(up.astype(F32) * attended[:, cols].astype(F32), axis=1, keepdims=True)
            scores = contract((q * scale).astype(BF), key, 1, 1) + bias_v[...]
            prob = jnp.exp(scores - totals[:, h : h + 1])
            grad_prob = contract(up, value, 1, 1)
            grad_scores = (prob * ((grad_prob - row_dot) * scale)).astype(BF)
            query_grad[:, cols] = jnp.dot(grad_scores, key, preferred_element_type=F32)
            key_sum += contract(grad_scores, q, 0, 0)
            value_sum += contract(prob.astype(BF), up, 0, 0)
        grads_v[:, g * HEAD : (g + 1) * HEAD] = key_sum
        grads_v[:, kv_width + g * HEAD : kv_width + (g + 1) * HEAD] = value_sum
    kv_grad[...] = grads_v[:rows, :]
    cols = kv_width // m
    for i in range(1, m):
        here = grads_v[i * rows : (i + 1) * rows, :]
        order = [offsets.index(p ^ offsets[i]) for p in offsets]
        pieces = [here[:, low + j * cols : low + (j + 1) * cols] for low in (0, kv_width) for j in order]
        kv_sends[i - 1][...] = jnp.concatenate(pieces, axis=1).astype(BF)


def join_grads_kernel(m, q_cols, kv_cols, place, query_grad, kv_grad, cosine, sine, *refs):
    received, outs = refs[: m - 1], refs[m - 1 :]
    kv_width = m * kv_cols
    cos, sin = cosine[...], sine[...]
    total = kv_grad[...]
    for piece in received:
        total += piece[...].astype(F32)
    keys = turn_heads(total[:, :kv_width], cos, sin, -1.0).astype(BF)
    values = total[:, kv_width:].astype(BF)
    for j in range(m):
        turned = turn_heads(query_grad[:, j * q_cols : (j + 1) * q_cols], cos, sin, -1.0)
        outs[j][:, :q_cols] = turned.astype(BF)
        outs[j][:, q_cols : q_cols + kv_cols] = keys[:, j * kv_cols : (j + 1) * kv_cols]
        outs[j][:, q_cols + kv_cols :] = values[:, j * kv_cols : (j + 1) * kv_cols]


def qkv_grad_kernel(n, k, place, normed, grads, *outs):
    block = normed.shape[1] // n
    for i in range(n):
        r = (1 + i) % n
        total = contract(normed[:, at(place, 1 + n + k + r, block)], grads[...], 0, 0)
        outs[r][...] = total.astype(outs[r].dtype)


def qkv_back_kernel(n, m, place, *refs):
    grads, weights, low, high = refs[:m], refs[m : m + n * m], refs[m + n * m], refs[m + n * m + 1]
    block = low.shape[1] // n
    half = low.shape[0]
    for r in range(n):
        total = 0.0
        for j in range(m):
            total += contract(grads[j][...], weights[r * m + j][...], 1, 1)
        low[:, at(place, 1 + r, block)] = total[:half]
        high[:, at(place, 1 + r, block)] = total[half:].astype(BF)


def qkv_join_kernel(m, offsets, q_cols, kv_cols, place, *refs):
    pieces, outs = refs[:m], refs[m:]
    me = place[0]
    for index in range(m):
        chosen = pieces[0][...].astype(F32)
        for j in range(1, m):
            chosen = jnp.where((me ^ offsets[j]) == index, pieces[j][...].astype(F32), chosen)
        low = 0
        for out, cols in zip(outs, (q_cols, kv_cols, kv_cols)):
            out[:, index * cols : (index + 1) * cols] = chosen[:, low : low + cols]
            low += cols


def local(
    hidden_in,
    cotangent,
    segment_ids,
    positions,
    attention_gain,
    query_weight,
    key_weight,
    value_weight,
    output_weight,
    feed_gain,
    gate_weight,
    up_weight,
    down_weight,
):
    n = lax.axis_size(SH)
    m = lax.axis_size(CX)
    k = lax.axis_size(TN)
    shard = lax.axis_index(SH)
    ctx = lax.axis_index(CX)
    ten = lax.axis_index(TN)
    t_offsets = xor_offsets(k)
    c_offsets = xor_offsets(m)
    _, rows, width = hidden_in.shape
    share = rows // k
    block = width // n
    place = scalars(
        ctx,
        *[(shard - r) % n for r in range(n)],
        *[ten ^ o for o in t_offsets],
        *[shard ^ o for o in range(n)],
    )
    ring_places = scalars(*[(shard - (shard ^ o)) % n for o in range(n)])
    hidden, cot = hidden_in[0], cotangent[0]

    kv_part = key_weight.shape[1] // HEAD // m
    q_cols = query_weight.shape[1] // m
    kv_cols = kv_part * HEAD
    part_cols = q_cols + 2 * kv_cols
    qkv_parts = pick_parts((query_weight, key_weight, value_weight), m)
    qkv_w = [qkv_parts]
    piece = qkv_parts[0]
    for r in range(1, n):
        piece = shift(piece, 1)
        qkv_w.append(gather_direct(piece))
        if r == max(n - 2, 1):
            middle_piece = piece
    if n == 1:
        middle_piece = piece
    gains = after(jnp.stack([attention_gain, feed_gain]), qkv_parts[0])
    gains = turn_blocks(jnp.concatenate([gains] + [shift(gains, r) for r in range(1, n)], axis=1), 1)

    units_mine = spread_units(place, gate_weight, up_weight, down_weight, n, m)
    unit_w = [list(units_mine[:m])]
    cot_pieces = [
        lax.dynamic_slice_in_dim(cot, (ten ^ o) * share, share, 0) for o in t_offsets
    ]
    hidden_own = own_part(hidden, TN, 0)
    out_mine = own_part(output_weight, CX, 0)
    inverse_freq = ROPE_BASE ** (-(jnp.arange(HEAD // 2, dtype=F32) * 2.0 / HEAD))
    place_rows = jnp.concatenate(
        [lax.dynamic_slice_in_dim(positions[0], (ten ^ o) * share, share, 0) for o in t_offsets]
    )
    reps = m * kv_cols // (HEAD // 2)
    angles = place_rows.astype(F32)[:, None] * jnp.tile(inverse_freq, reps)[None, :]
    signs = jnp.tile(jnp.repeat(jnp.array([-1.0, 1.0], F32), HEAD // 2), reps // 2)
    cosine, sine = jnp.cos(angles), jnp.sin(angles) * signs[None, :]
    seg_row = segment_ids
    seg_col = segment_ids.reshape(-1, 1)

    normed_one = call(lambda *refs: norm_kernel(n, k, *refs), shaped((rows, width), BF), (place, hidden, gains))
    out_mine = after(out_mine, middle_piece)
    out_firsts = []
    for r in range(1, n):
        out_firsts.append(shift(out_mine, r))
    flat_qkv = [w for parts in qkv_w for w in parts]
    query, kv_own, *kv_sends = call(
        lambda *refs: qkv_kernel(n, m, q_cols, kv_cols, *refs),
        [shaped((rows, m * q_cols), BF)] + [shaped((rows, 2 * m * kv_cols), BF)] * m,
        (place, normed_one, cosine, sine, *flat_qkv),
    )
    early_values = lax.optimization_barrier((kv_own, hidden_own, *cot_pieces, seg_col, middle_piece))
    kv_own, hidden_own, cot_pieces, seg_col = (
        early_values[0],
        early_values[1],
        list(early_values[2 : 2 + k]),
        early_values[2 + k],
    )
    kv_others = []
    for o, sent in zip(c_offsets[1:], kv_sends):
        kv_others.append(swap(sent, CX, o))
    out_stack = after(jnp.stack(out_firsts), kv_own)
    out_others = []
    for o in c_offsets[1:]:
        out_others.append(swap(out_stack, CX, o))
    units_sent = list(units_mine[m:])
    early = [r for r in range(1, n) if r != n // 2]
    moved = [None] * n
    for r in early:
        moved[r] = shift(units_sent[r - 1] if r == 1 else after(units_sent[r - 1], out_stack), r)
    wide = 2 * m * kv_cols
    attended, totals = call(
        lambda *refs: attend_kernel(n, m, k, *refs),
        [shaped((rows, m * q_cols), BF), shaped((rows, 128), F32)],
        (place, query, seg_row, seg_col, kv_own, *kv_others),
        [pltpu.VMEM((rows, m * rows), F32), pltpu.VMEM((m * rows, wide), BF)],
    )
    for r in range(1, n):
        if r not in early:
            moved[r] = shift(after(units_sent[r - 1], attended), r)
    low, high = call(
        lambda *refs: out_kernel(n, m, *refs),
        [shaped((rows // 2, width), F32), shaped((rows // 2, width), BF)],
        (place, attended, output_weight, *out_firsts, *out_others),
    )

    def scatter_open(low, high):
        bits = xor_bits(k)
        for i, bit in enumerate(bits):
            received = swap(high, TN, bit)
            if i + 1 < len(bits):
                total = low.astype(F32) + received.astype(F32)
                half = total.shape[-2] // 2
                low, high = total[..., :half, :], total[..., half:, :].astype(BF)
        return low, received

    kept, received = scatter_open(low, high)
    residual, normed_two, stream_own = call(
        residual_kernel,
        [shaped((share, width), F32), shaped((share, width), BF), shaped((2 * share, width), BF)],
        (place, kept, received, hidden_own, gains, cot_pieces[0]),
    )

    stream = [stream_own if n == 1 else after(stream_own, moved[n // 2])]
    for r in range(1, n):
        stream.append(shift(stream[-1], 1))
    for r in range(1, n):
        unit_w.append(gather_direct(after(moved[r], attended if r == 1 else normed_two)))
    flat_units = [w for parts in unit_w for w in parts]
    carried = None
    back_kept = []
    back_received = []
    for r in range(n):
        acts = [stream[r] if r else normed_two]
        for bit in reversed(xor_bits(k)):
            acts = acts + [swap(p, TN, bit) for p in acts]
        carried, low, high = mlp_chunk(
            r, n, m, place, acts, [] if r else cot_pieces, flat_units, carried
        )
        kept, received = scatter_open(low, high)
        back_kept.append(kept)
        back_received.append(received)
    back_moved = []
    for r in range(1, n):
        part = (back_kept[r] + back_received[r].astype(F32)).astype(BF)
        back_moved.append(shift(part, -r))
    grad_residual, grad_b, gain_two_term = call(
        feed_back_kernel,
        [shaped((share, width), F32), shaped((share, width), BF), shaped((1, width), F32)],
        (place, back_kept[0], back_received[0], residual, gains, cot_pieces[0], *back_moved),
    )
    all_acts, all_cots, all_hid, all_back = carried[0], carried[1], carried[2 : 2 + m], carried[2 + m :]

    def send_part(value, j):
        return swap(value.astype(BF), CX, c_offsets[j])

    unit_terms = [[] for _ in range(n)]
    for j in reversed(range(m)):
        half = n // 2 if j else n
        parts = [None] * n
        for first in range(1, n + 1, half):
            some = unit_grads(
                place, all_acts, all_cots, all_hid[j], all_back[j],
                BF if j else F32, n, first, half,
            )
            for i, value in enumerate(some):
                parts[(first + i) % n] = value
        for i in range(n):
            r = (1 + i) % n
            if j:
                parts[r] = send_part(parts[r], j)
            unit_terms[r].append(parts[r])
    unit_totals = []
    for r in range(n):
        total = sum(t.astype(F32) for t in unit_terms[r]).astype(BF)
        if r:
            total = shift(total, -r)
        unit_totals.append(total)
    grads = [grad_b]
    for bit in reversed(xor_bits(k)):
        grads = grads + [swap(p, TN, bit) for p in grads]
    feed_low, feed_high = feed_out(place, [after(h, grad_b) for h in all_hid], flat_units, rows, n)
    attended_grad, all_grads = call(
        lambda *refs: out_back_kernel(n, m, k, *refs),
        [shaped((rows, m * q_cols), BF), shaped((rows, width), BF)],
        (place, output_weight, *grads, *out_firsts, *out_others),
    )
    query_grad, kv_grad, *kv_sends = call(
        lambda *refs: attend_back_kernel(n, m, k, *refs),
        [shaped((rows, m * q_cols), F32), shaped((rows, wide), F32)]
        + [shaped((rows, wide), BF)] * (m - 1),
        (place, query, seg_row, seg_col, attended, attended_grad, totals, kv_own, *kv_others),
        [
            pltpu.VMEM((rows, m * rows), F32),
            pltpu.VMEM((m * rows, wide), BF),
            pltpu.VMEM((m * rows, wide), F32),
        ],
    )
    kv_received = []
    for o, sent in zip(c_offsets[1:], kv_sends):
        kv_received.append(swap(sent, CX, o))
    out_grads = call(
        lambda *refs: out_grad_kernel(n, m, k, *refs),
        [shaped((m * q_cols, block), BF if r % 2 else F32) for r in range(n)],
        (place, attended, after(all_grads, kv_grad)),
    )
    feed_bits = xor_bits(k)
    assert len(feed_bits) == 2
    for i, bit in enumerate(feed_bits):
        if i + 1 == len(feed_bits):
            feed_high = after(feed_high, kv_grad)
        feed_received = swap(feed_high, TN, bit)
        if i + 1 < len(feed_bits):
            feed_low, feed_high = feed_add(ring_places, feed_low, feed_received)
    feed_sum = feed_low.astype(F32) + feed_received.astype(F32)
    total = shard_sum([feed_sum[o] for o in range(n)])
    layer_out = (residual + total).astype(BF)[None]

    qkv_grads = call(
        lambda *refs: join_grads_kernel(m, q_cols, kv_cols, *refs),
        [shaped((rows, part_cols), BF)] * m,
        (place, query_grad, kv_grad, cosine, sine, *kv_received),
    )
    terms = [[] for _ in range(n)]
    for j in reversed(range(m)):
        parts = list(call(
            lambda *refs: qkv_grad_kernel(n, k, *refs),
            [shaped((block, part_cols), BF if j else F32)] * n,
            (place, normed_one, qkv_grads[j]),
        ))
        for r in list(range(1, n, 2)) + list(range(0, n, 2)):
            if j:
                parts[r] = send_part(parts[r], j)
            terms[r].append(parts[r])
    total = shard_sum(out_grads)
    parts = [total[j * q_cols : (j + 1) * q_cols] for j in range(m)]
    sums = list(parts)
    for o in c_offsets[1:]:
        order = [c_offsets.index(p ^ o) for p in c_offsets]
        got = swap(jnp.concatenate([parts[i] for i in order]).astype(BF), CX, o)
        sums = [s + got[j * q_cols : (j + 1) * q_cols].astype(F32) for j, s in enumerate(sums)]
    grad_output_out = join_rows([s[None] for s in sums])
    unit_parts = []
    for r in range(n):
        unit_parts.append(gather_direct(after(unit_totals[r], terms[0][-1] if r > 1 else grad_b)))
    low, high = call(
        lambda *refs: qkv_back_kernel(n, m, *refs),
        [shaped((rows // 2, width), F32), shaped((rows // 2, width), BF)],
        (place, *qkv_grads, *flat_qkv),
    )
    kept, received = scatter_open(low, high)
    total = shard_sum([sum(t.astype(F32) for t in term) for term in terms])
    qkv_parts_out = gather_direct(total.astype(BF))
    grad_query_out, grad_key_out, grad_value_out = call(
        lambda *refs: qkv_join_kernel(m, c_offsets, q_cols, kv_cols, *refs),
        [shaped((block, m * cols), F32) for cols in (q_cols, kv_cols, kv_cols)],
        (place, *qkv_parts_out),
    )
    grad_input, gain_one_term = call(
        input_back_kernel,
        [shaped((share, width), F32), shaped((1, width), F32)],
        (place, kept, received, hidden_own, gains, grad_residual),
    )
    gain_one, gain_two = gain_total(jnp.concatenate([gain_one_term, gain_two_term]))
    joined = None
    for r in range(n):
        joined = join_units(place, r, n, unit_parts[r], joined)
    grad_gate_out, grad_up_out, grad_down_out = joined
    return (
        layer_out,
        grad_input[None],
        gain_one,
        grad_query_out,
        grad_key_out,
        grad_value_out,
        grad_output_out,
        gain_two,
        grad_gate_out,
        grad_up_out,
        grad_down_out,
    )


def solution(mesh):
    placed = (
        P(SH, CX, None),
        P(SH, CX, None),
        P(SH, None),
        P(SH, CX),
        P(SH),
        P(SH, TN),
        P(SH, TN),
        P(SH, TN),
        P(TN, SH),
        P(SH),
        P(SH, TN),
        P(SH, TN),
        P(TN, SH),
    )

    return jax.shard_map(
        local,
        mesh=mesh,
        in_specs=placed,
        out_specs=(
            P(SH, (CX, TN), None),
            P(SH, (CX, TN), None),
            P(SH),
            P(SH, TN),
            P(SH, TN),
            P(SH, TN),
            P(TN, SH),
            P(SH),
            P(SH, TN),
            P(SH, TN),
            P(TN, SH),
        ),
        check_vma=False,
    )
```
